256 devices in a mesh: lat: 4 (over x_hi, core), lon: 64 (over z, x_lo, y).
Axes of the slice: x: 4 (x_hi: 2, x_lo: 2; x = x_hi * 2 + x_lo), y: 4, z: 8, core: 2. Of those that a mesh axis runs over, the one named last changes fastest.
Arguments:
- tendencies: bfloat16 [3, 64, 2880, 128], P(None, 'lat', 'lon'), may hold values from -6 to 6
- bands: int32 [64], replicated, may hold values from 45 to 180
- winds: float32 [2, 64, 2880, 128], P(None, 'lat', 'lon'), may hold values from -6 to 6
- tracers: float32 [5, 64, 2880, 128], P(None, 'lat', 'lon'), may hold values from -6 to 6
Outputs:
- filtered: bfloat16 [3, 64, 2880, 128], P(None, 'lat', 'lon')
- advected: float32 [5, 64, 2880, 128], P(None, 'lat', 'lon')
The draws below stay inside these ranges and needn't reach their ends.
All inputs are finite; a program needn't handle non-finite values.
Results may differ from the reference program's by a relative error of at most 0.0038.
Values may be sent and summed in bfloat16 or wider, within the bound.
No kernel may reach another device: no remote copies, remote signals or barrier semaphores. Data moves between devices by JAX's collectives and lax.ppermute only.
A program may use at most 64 MiB of HBM per device.

```python
import jax
import jax.numpy as jnp
from jax import lax

NLON = 2880
HEMI = 720
LEV = 128
FIELDS = 3
TRACERS = 5
NLAT = 64
J0 = 328


def plant(array, own_key, smallest, high):
    longest = array.shape.index(max(array.shape))
    spots = []
    for shift in (0, 1):
        where = [jax.random.randint(jax.random.fold_in(own_key, axis), (), 0, length) for axis, length in enumerate(array.shape)]
        where[longest] = (where[longest] + shift) % array.shape[longest]
        spots.append(tuple(where))
    return array.at[spots[0]].set(smallest).at[spots[1]].set(high)


def level_of(rng, dims, split, low, high):
    level, own = 1.0, jax.random.fold_in(rng, 6)
    for dim, shards_of in split:
        draws = jnp.exp(jax.random.uniform(jax.random.fold_in(own, dim), (shards_of,), jnp.float32, low / len(split), high / len(split)))
        level = level * jnp.repeat(draws, dims[dim] // shards_of).reshape([-1 if axis == dim else 1 for axis in range(len(dims))])
    return level


def bell_draw(own_key, dims, scale, reach, cuts=(), held_as=jnp.bfloat16):
    drawn = jax.random.normal(own_key, dims, jnp.float32) * scale
    if len(cuts) > 0:
        drawn = level_of(own_key, dims, cuts, -0.22, 0.18) * drawn
    return jnp.clip(drawn, min=-reach, max=reach).astype(held_as)


def setup_inputs(seed: int = 0) -> dict:
    arg_keys = jax.random.split(jax.random.key(seed), 5)
    return {
        "tendencies": bell_draw(arg_keys[0], (FIELDS, NLAT, NLON, LEV), 1.0, 6.0, ((1, 4), (2, 64))),
        "bands": plant(jax.random.randint(arg_keys[1], (NLAT,), NLON // 64, NLON // 16 + 1), jax.random.fold_in(arg_keys[1], 1), NLON // 64, (NLON // 16 + 1) - 1).astype(jnp.int32),
        "winds": bell_draw(arg_keys[2], (2, NLAT, NLON, LEV), 1.0, 6.0, ((1, 4), (2, 64)), jnp.float32),
        "tracers": bell_draw(arg_keys[3], (TRACERS, NLAT, NLON, LEV), 1.0, 6.0, ((1, 4), (2, 64)), jnp.float32),
    }


def reference(tendencies, bands, winds, tracers):
    lat_count = tendencies.shape[1]
    lon_count = tendencies.shape[2]
    half_wave = lon_count // 2
    row_index = jnp.arange(lat_count, dtype=jnp.float32)
    grid_row = row_index + jnp.float32(J0)
    centre_cos = jnp.sin(jnp.pi * (grid_row + 0.5) / (2.0 * HEMI))
    face_cos = jnp.sin(jnp.pi * grid_row / (2.0 * HEMI))
    damping = 0.25 + 0.5 * (row_index + 0.5) / (lat_count / 2.0)
    wave_index = jnp.arange(half_wave + 1, dtype=jnp.int32)
    polar_rows = jnp.arange(lat_count, dtype=jnp.int32) < lat_count // 2
    retained = (wave_index[None, :] <= bands[:, None]) | jnp.logical_not(polar_rows[:, None])
    multiplier = jnp.where(retained, jnp.float32(1.0), damping[:, None]).astype(jnp.float32)

    def filter_field(one_field):
        spectrum = jnp.fft.rfft(one_field.astype(jnp.float32), axis=1)
        return jnp.fft.irfft(spectrum * multiplier[:, :, None], n=lon_count, axis=1).astype(jnp.float32)

    filtered = lax.map(filter_field, tendencies).astype(jnp.bfloat16)
    new_winds = winds + filtered[0:2].astype(jnp.float32)
    east_courant = 0.5 * jnp.tanh(new_winds[0])
    north_courant = 0.25 * jnp.tanh(new_winds[1])
    west_cells = jnp.roll(tracers, 1, axis=2)
    f_west = jnp.maximum(east_courant, 0.0) * west_cells + jnp.minimum(east_courant, 0.0) * tracers
    f_east = jnp.roll(f_west, -1, axis=2)
    prior_rows = jnp.concatenate([jnp.zeros_like(tracers[:, :1]), tracers[:, :-1]], axis=1)
    g_pole = face_cos[:, None, None] * (jnp.maximum(north_courant, 0.0) * prior_rows + jnp.minimum(north_courant, 0.0) * tracers)
    g_next = jnp.concatenate([g_pole[:, 1:], jnp.zeros_like(g_pole[:, :1])], axis=1)
    advected = tracers - (f_east - f_west) - (g_next - g_pole) / centre_cos[:, None, None]
    return filtered, advected
```

```python
import math

import jax
import jax.numpy as jnp
import numpy as np
from jax import lax
from jax.experimental import pallas as pl
from jax.experimental.pallas import tpu as pltpu
from jax.sharding import PartitionSpec as P

HEMI = 720
KMAX = 180
COEF = 384
SEG = 48
COLS = 9


def trig_tables(lon_count, segments):
    width = lon_count // segments
    k = np.zeros(COEF)
    k[: KMAX + 1] = np.arange(KMAX + 1)
    k[KMAX + 1 : 2 * KMAX + 1] = np.arange(1, KMAX + 1)
    is_cos = np.zeros(COEF, bool)
    is_cos[: KMAX + 1] = True
    used = np.arange(COEF) < 2 * KMAX + 1
    over_p = 2 * np.pi * np.outer(np.arange(segments) * width, k) / lon_count
    over_q = 2 * np.pi * np.outer(np.arange(SEG), k) / lon_count
    p_one = np.where(is_cos, np.cos(over_p), np.sin(over_p)) * used
    p_two = np.where(is_cos, -np.sin(over_p), np.cos(over_p)) * used
    tables = (p_one, p_two, np.cos(over_q), np.sin(over_q))
    return tuple(t.astype(np.float32) for t in tables), k.astype(np.int32), used


def pack_kernel(tend_ref, next_ref, out_ref, wide_ref):
    fields, width, lat_rows, levels = tend_ref.shape
    slots = fields * lat_rows
    pad = out_ref.shape[1] - width
    for f in range(fields):
        wide_ref[...] = tend_ref[f].astype(jnp.float32).reshape(width * lat_rows, levels)
        for r in range(lat_rows):
            row = wide_ref[pl.ds(r, width, stride=lat_rows), :]
            out_ref[f * lat_rows + r, :width] = row.astype(jnp.bfloat16)
            out_ref[f * lat_rows + r, width:] = jnp.zeros((pad, levels), jnp.bfloat16)
    out_ref[slots, :width] = next_ref[...]
    out_ref[slots, width:] = jnp.zeros((pad, levels), jnp.bfloat16)
    for s in range(slots + 1, out_ref.shape[0]):
        out_ref[s] = jnp.zeros(out_ref.shape[1:], jnp.bfloat16)


def transform_kernel(rows_ref, table_ref, weight_ref, out_ref):
    spectrum = lax.dot_general(
        rows_ref[...], table_ref[...], (((0,), (0,)), ((), ())), preferred_element_type=jnp.float32
    )
    weighted = (spectrum * weight_ref[...]).astype(jnp.bfloat16)
    out_ref[...] = lax.dot_general(
        table_ref[...], weighted, (((1,), (1,)), ((), ())), preferred_element_type=jnp.float32
    ).astype(jnp.bfloat16)


def advect_kernel(
    low_ref,
    factor_ref,
    tend_ref,
    wind_ref,
    tracer_ref,
    before_ref,
    high_ref,
    side_ref,
    below_ref,
    top_ref,
    filt_ref,
    out_ref,
    wide_ref,
    north_ref,
    flux_ref,
):
    step = pl.program_id(0)
    block = pl.num_programs(0) - 1 - step
    count, _, lat_rows, levels = tracer_ref.shape
    width = below_ref.shape[1]
    damp, face, face_next, inverse = (factor_ref[i] for i in range(4))
    sublane = lax.broadcasted_iota(jnp.int32, (lat_rows, levels), 0)
    is_first = sublane == 0
    is_last = sublane == lat_rows - 1

    def low_at(f, column):
        start = pl.multiple_of((f * SEG + column) * lat_rows, lat_rows)
        return wide_ref[pl.ds(start, lat_rows), :]

    @pl.when(step == 0)
    def _():
        for f in range(3):
            for r in range(lat_rows):
                wide_ref[pl.ds(f * SEG * lat_rows + r, SEG, stride=lat_rows), :] = low_ref[
                    f * lat_rows + r
                ].astype(jnp.float32)
        filt = (
            factor_ref[4, 0:1] * below_ref[count + 1] + low_ref[3 * lat_rows, :width].astype(jnp.float32)
        ).astype(jnp.bfloat16)
        north_ref[0:width] = 0.25 * jnp.tanh(below_ref[count] + filt.astype(jnp.float32))
        filt = (damp * high_ref[count + 1] + low_at(0, width)).astype(jnp.bfloat16)
        east = 0.5 * jnp.tanh(high_ref[count] + filt.astype(jnp.float32))
        for q in range(count):
            flux_ref[q] = (
                jnp.maximum(east, 0.0) * tracer_ref[q, COLS - 1] + jnp.minimum(east, 0.0) * high_ref[q]
            )

    for local in reversed(range(COLS)):
        column = block * COLS + local
        filtered = []
        for f in range(3):
            value = (damp * tend_ref[f, local].astype(jnp.float32) + low_at(f, column)).astype(
                jnp.bfloat16
            )
            filt_ref[f, local] = value
            filtered.append(value)
        east = 0.5 * jnp.tanh(wind_ref[0, local] + filtered[0].astype(jnp.float32))
        north = 0.25 * jnp.tanh(wind_ref[1, local] + filtered[1].astype(jnp.float32))
        north_next = jnp.where(
            is_last, north_ref[pl.ds(column, 1), :], pltpu.roll(north, lat_rows - 1, 0)
        )
        west_plus = jnp.maximum(east, 0.0)
        west_minus = jnp.minimum(east, 0.0)
        pole_plus = face * jnp.maximum(north, 0.0)
        pole_minus = face * jnp.minimum(north, 0.0)
        next_plus = face_next * jnp.maximum(north_next, 0.0)
        next_minus = face_next * jnp.minimum(north_next, 0.0)
        for q in range(count):
            here = tracer_ref[q, local]
            if local > 0:
                west = tracer_ref[q, local - 1]
            else:
                west = jnp.where(block == 0, side_ref[q], before_ref[q, 0])
            prior = jnp.where(is_first, top_ref[q, pl.ds(column, 1), :], pltpu.roll(here, 1, 0))
            after = jnp.where(
                is_last, below_ref[q, pl.ds(column, 1), :], pltpu.roll(here, lat_rows - 1, 0)
            )
            f_east = flux_ref[q]
            f_west = west_plus * west + west_minus * here
            flux_ref[q] = f_west
            g_pole = pole_plus * prior + pole_minus * here
            g_next = next_plus * here + next_minus * after
            out_ref[q, local] = here - (f_east - f_west) - (g_next - g_pole) * inverse


def per_device(tendencies, bands, winds, tracers):
    fields, lat_rows, width, levels = tendencies.shape
    count = tracers.shape[0]
    lat_devices = lax.axis_size("lat")
    segments = lax.axis_size("lon")
    lat_count = lat_devices * lat_rows
    lon_count = segments * width
    lat_place = lax.axis_index("lat")
    lon_place = lax.axis_index("lon")
    slots = fields * lat_rows
    tendencies, winds, tracers = (a.transpose(0, 2, 1, 3) for a in (tendencies, winds, tracers))

    to_prior = [(i + 1, i) for i in range(lat_devices - 1)]
    to_next = [(i, i + 1) for i in range(lat_devices - 1)]
    west_ring = [((i + 1) % segments, i) for i in range(segments)]
    east_ring = [(i, (i + 1) % segments) for i in range(segments)]

    next_row = lax.ppermute(tendencies[1, :, 0], "lat", to_prior)
    send = pl.pallas_call(
        pack_kernel,
        out_shape=jax.ShapeDtypeStruct((segments, SEG, levels), jnp.bfloat16),
        scratch_shapes=[pltpu.VMEM((width * lat_rows, levels), jnp.float32)],
        name="pack",
    )(tendencies, next_row)
    rows = lax.all_to_all(send, "lon", split_axis=0, concat_axis=0, tiled=True)

    ids = lat_place * lat_rows + jnp.arange(lat_rows + 1, dtype=jnp.int32)
    position = ids.astype(jnp.float32)
    polar = ids < lat_count // 2
    damping = jnp.where(polar, 0.25 + 0.5 * (position + 0.5) / (lat_count / 2.0), 1.0)
    grid_row = position + jnp.float32(HEMI // 2 - lat_count // 2)
    face_cos = jnp.sin(math.pi * grid_row / (2.0 * HEMI))
    centre_cos = jnp.sin(math.pi * (grid_row + 0.5) / (2.0 * HEMI))
    factors = jnp.stack(
        [
            damping[:lat_rows],
            face_cos[:lat_rows],
            face_cos[1:],
            1.0 / centre_cos[:lat_rows],
            jnp.full((lat_rows,), damping[lat_rows]),
        ]
    )
    factors = jnp.broadcast_to(factors[:, :, None], (5, lat_rows, levels))

    (p_one, p_two, q_one, q_two), waves, used = trig_tables(lon_count, segments)
    mine = jnp.where(lon_place < slots, lon_place % lat_rows, lat_rows)
    my_id = lat_place * lat_rows + mine
    my_band = bands[jnp.minimum(my_id, lat_count - 1)]
    fold = jnp.asarray(np.where(used, np.where(waves == 0, 1.0, 2.0), 0.0) / lon_count, jnp.float32)
    weight = jnp.where(jnp.asarray(waves) <= my_band, (1.0 - damping[mine]) * fold, 0.0)[None, :]
    table = (
        jnp.asarray(p_one)[:, None, :] * jnp.asarray(q_one)[None, :, :]
        + jnp.asarray(p_two)[:, None, :] * jnp.asarray(q_two)[None, :, :]
    )
    table = table.astype(jnp.bfloat16).reshape(segments * SEG, COEF)

    high = jnp.concatenate(
        [tracers[:, 0], winds[0:1, 0], tendencies[0:1, 0].astype(jnp.float32)], axis=0
    )
    high = lax.ppermute(high.astype(jnp.bfloat16), "lon", west_ring).astype(jnp.float32)
    side = lax.ppermute(tracers[:, width - 1].astype(jnp.bfloat16), "lon", east_ring)
    side = side.astype(jnp.float32)
    below = jnp.concatenate([tracers[:, :, 0], winds[1:2, :, 0]], axis=0).astype(jnp.bfloat16)
    below = lax.ppermute(below, "lat", to_prior)
    below = jnp.concatenate([below, next_row[None]], axis=0).astype(jnp.float32)
    top = lax.ppermute(tracers[:, :, lat_rows - 1].astype(jnp.bfloat16), "lat", to_next)
    top = top.astype(jnp.float32)

    low = pl.pallas_call(
        transform_kernel,
        out_shape=jax.ShapeDtypeStruct((segments * SEG, levels), jnp.bfloat16),
        name="transform",
    )(rows.reshape(segments * SEG, levels), table, weight)
    low = lax.all_to_all(
        low.reshape(segments, SEG, levels), "lon", split_axis=0, concat_axis=0, tiled=True
    )

    blocks = width // COLS

    def whole(array):
        return pl.BlockSpec(array.shape, lambda i: (0,) * array.ndim)

    def part(size):
        return pl.BlockSpec((size, COLS, lat_rows, levels), lambda i: (0, blocks - 1 - i, 0, 0))

    filtered, advected = pl.pallas_call(
        advect_kernel,
        grid=(blocks,),
        in_specs=[
            whole(low),
            whole(factors),
            part(fields),
            part(2),
            part(count),
            pl.BlockSpec(
                (count, 1, lat_rows, levels),
                lambda i: (0, jnp.maximum((blocks - 1 - i) * COLS - 1, 0), 0, 0),
            ),
            whole(high),
            whole(side),
            whole(below),
            whole(top),
        ],
        out_specs=[part(fields), part(count)],
        out_shape=[
            jax.ShapeDtypeStruct(tendencies.shape, jnp.bfloat16),
            jax.ShapeDtypeStruct(tracers.shape, jnp.float32),
        ],
        scratch_shapes=[
            pltpu.VMEM((fields * SEG * lat_rows, levels), jnp.float32),
            pltpu.VMEM((SEG, levels), jnp.float32),
            pltpu.VMEM((count, lat_rows, levels), jnp.float32),
        ],
        name="advect",
    )(low, factors, tendencies, winds, tracers, tracers, high, side, below, top)
    return (filtered.transpose(0, 2, 1, 3), advected.transpose(0, 2, 1, 3))


def solution(mesh):
    return jax.shard_map(
        per_device,
        mesh=mesh,
        in_specs=(
            P(None, "lat", "lon", None),
            P(),
            P(None, "lat", "lon", None),
            P(None, "lat", "lon", None),
        ),
        out_specs=(P(None, "lat", "lon", None), P(None, "lat", "lon", None)),
        check_vma=False,
    )
```

```python
import math

import jax
import jax.numpy as jnp
import numpy as np
from jax import lax
from jax.experimental import pallas as pl
from jax.experimental.pallas import tpu as pltpu
from jax.sharding import PartitionSpec as P

HEMI = 720
KMAX = 180
COEF = 384
SEG = 48
LIMIT = 24 << 20
CHUNKS = 4
COLS = 9


def trig_tables(lon_count, segments):
    width = lon_count // segments
    k = np.zeros(COEF)
    k[: KMAX + 1] = np.arange(KMAX + 1)
    k[KMAX + 1 : 2 * KMAX + 1] = np.arange(1, KMAX + 1)
    is_cos = np.zeros(COEF, bool)
    is_cos[: KMAX + 1] = True
    used = np.arange(COEF) < 2 * KMAX + 1
    over_p = 2 * np.pi * np.outer(np.arange(segments) * width, k) / lon_count
    over_q = 2 * np.pi * np.outer(np.arange(SEG), k) / lon_count
    p_one = np.where(is_cos, np.cos(over_p), np.sin(over_p)) * used
    p_two = np.where(is_cos, -np.sin(over_p), np.cos(over_p)) * used
    tables = (p_one, p_two, np.cos(over_q), np.sin(over_q))
    return tuple(t.astype(np.float32) for t in tables), k.astype(np.int32), used


def pack_kernel(tend_ref, out_ref, tend, wide, rows, in_sems, out_sems):
    fields, width, lat_rows, levels = tend.shape
    pad = rows.shape[1] - width
    loads = [pltpu.make_async_copy(tend_ref.at[f], tend.at[f], in_sems.at[f]) for f in range(fields)]
    for load in loads:
        load.start()
    stores = []
    blocks = rows.shape[0] // lat_rows
    for f in reversed(range(blocks)):
        part = pl.ds(f * lat_rows, lat_rows)
        if f < fields:
            loads[f].wait()
            wide[f] = tend[f].astype(jnp.float32).reshape(width * lat_rows, levels)
            for r in range(lat_rows):
                row = wide[f, pl.ds(r, width, stride=lat_rows), :]
                rows[f * lat_rows + r, :width] = row.astype(jnp.bfloat16)
                rows[f * lat_rows + r, width:] = jnp.zeros((pad, levels), jnp.bfloat16)
        else:
            rows[part] = jnp.zeros((lat_rows,) + rows.shape[1:], jnp.bfloat16)
        store = pltpu.make_async_copy(rows.at[part], out_ref.at[part], out_sems.at[f])
        store.start()
        stores.append(store)
    for store in stores:
        store.wait()


def transform_kernel(
    place_ref, bands_ref, waves_ref, fold_ref, rows_ref, table_ref, out_ref, table, result, in_sems, out_sems
):
    row, half = place_ref[0], place_ref[1]
    damp = jnp.where(row < half, 0.25 + 0.5 * (row.astype(jnp.float32) + 0.5) / half.astype(jnp.float32), 1.0)
    weight = jnp.where(waves_ref[...] <= bands_ref[row], (1.0 - damp) * fold_ref[...], 0.0)
    size = table.shape[0] // CHUNKS

    def part(i):
        return pl.ds(i * size, size)

    loads = [
        pltpu.make_async_copy(table_ref.at[part(i)], table.at[part(i)], in_sems.at[i])
        for i in range(CHUNKS)
    ]
    stores = [
        pltpu.make_async_copy(result.at[part(i)], out_ref.at[part(i)], out_sems.at[i])
        for i in range(CHUNKS)
    ]
    for load in loads:
        load.start()
    spectrum = 0.0
    for i in range(CHUNKS):
        loads[i].wait()
        spectrum += lax.dot_general(
            rows_ref[part(i)],
            table[part(i)],
            (((0,), (0,)), ((), ())),
            preferred_element_type=jnp.float32,
        )
    weighted = (spectrum * weight).astype(jnp.bfloat16)
    for i in range(CHUNKS):
        result[part(i)] = lax.dot_general(
            table[part(i)], weighted, (((1,), (1,)), ((), ())), preferred_element_type=jnp.float32
        ).astype(jnp.bfloat16)
        stores[i].start()
    for store in stores:
        store.wait()


def filter_kernel(place_ref, low_ref, factor_ref, tend_ref, high_ref, filt_ref, edge_ref, wide_ref):
    fields, width, lat_rows, levels = tend_ref.shape
    damp = factor_ref[place_ref[2], 0]
    for f in range(fields):
        for r in range(lat_rows):
            wide_ref[f, pl.ds(r, SEG, stride=lat_rows), :] = low_ref[f * lat_rows + r].astype(jnp.float32)
        if f == 0:
            filt = damp * high_ref[high_ref.shape[0] - 1].astype(jnp.float32)
            filt += wide_ref[f, width * lat_rows : (width + 1) * lat_rows]
            filt = filt.astype(jnp.bfloat16).astype(jnp.float32)
            edge_ref[...] = 0.5 * jnp.tanh(high_ref[high_ref.shape[0] - 2].astype(jnp.float32) + filt)
        low = wide_ref[f, : width * lat_rows].reshape(width, lat_rows, levels)
        filt_ref[f] = (damp[None] * tend_ref[f].astype(jnp.float32) + low).astype(jnp.bfloat16)


def advect_kernel(
    place_ref,
    filt_ref,
    factor_ref,
    wind_ref,
    tracer_ref,
    before_ref,
    edge_ref,
    high_ref,
    side_ref,
    below_ref,
    top_ref,
    next_low_ref,
    out_ref,
    north_ref,
    flux_ref,
    below_wide,
    top_wide,
):
    step = pl.program_id(0)
    block = pl.num_programs(0) - 1 - step
    count, _, lat_rows, levels = tracer_ref.shape
    width = below_ref.shape[1]
    lat = place_ref[2]
    _, face, face_next, inverse = (factor_ref[lat, i] for i in range(4))
    sublane = lax.broadcasted_iota(jnp.int32, (lat_rows, levels), 0)
    is_first = sublane == 0
    is_last = sublane == lat_rows - 1

    @pl.when(step == 0)
    def _():
        below_wide[:, :width] = below_ref[...].astype(jnp.float32)
        top_wide[:, :width] = top_ref[...].astype(jnp.float32)
        filt = factor_ref[lat, 4, 0:1] * below_wide[count + 1, :width]
        filt = (filt + next_low_ref[:width].astype(jnp.float32)).astype(jnp.bfloat16)
        north_ref[:width] = 0.25 * jnp.tanh(below_wide[count, :width] + filt.astype(jnp.float32))
        east = edge_ref[...]
        for q in range(count):
            flux_ref[q] = jnp.maximum(east, 0.0) * tracer_ref[q, COLS - 1] + jnp.minimum(
                east, 0.0
            ) * high_ref[q].astype(jnp.float32)

    for local in reversed(range(COLS)):
        column = block * COLS + local
        east = 0.5 * jnp.tanh(wind_ref[0, local] + filt_ref[0, local].astype(jnp.float32))
        north = 0.25 * jnp.tanh(wind_ref[1, local] + filt_ref[1, local].astype(jnp.float32))
        north_next = jnp.where(
            is_last, north_ref[pl.ds(column, 1), :], pltpu.roll(north, lat_rows - 1, 0)
        )
        west_plus = jnp.maximum(east, 0.0)
        west_minus = jnp.minimum(east, 0.0)
        pole_plus = face * jnp.maximum(north, 0.0)
        pole_minus = face * jnp.minimum(north, 0.0)
        next_plus = face_next * jnp.maximum(north_next, 0.0)
        next_minus = face_next * jnp.minimum(north_next, 0.0)
        for q in range(count):
            here = tracer_ref[q, local]
            if local > 0:
                west = tracer_ref[q, local - 1]
            else:
                west = jnp.where(block == 0, side_ref[q].astype(jnp.float32), before_ref[q, 0])
            prior = jnp.where(is_first, top_wide[q, pl.ds(column, 1), :], pltpu.roll(here, 1, 0))
            after = jnp.where(
                is_last, below_wide[q, pl.ds(column, 1), :], pltpu.roll(here, lat_rows - 1, 0)
            )
            f_east = flux_ref[q]
            f_west = west_plus * west + west_minus * here
            flux_ref[q] = f_west
            g_pole = pole_plus * prior + pole_minus * here
            g_next = next_plus * here + next_minus * after
            out_ref[q, local] = here - (f_east - f_west) - (g_next - g_pole) * inverse


def row_factors(lat_devices, lat_rows, levels):
    ids = np.arange(lat_devices * lat_rows + 1)
    half = lat_devices * lat_rows // 2
    damping = np.where(ids < half, 0.25 + 0.5 * (ids + 0.5) / half, 1.0)
    grid_row = ids + HEMI // 2 - half
    face = np.sin(math.pi * grid_row / (2.0 * HEMI))
    centre = np.sin(math.pi * (grid_row + 0.5) / (2.0 * HEMI))
    rows = np.stack(
        [damping[:-1], face[:-1], face[1:], 1.0 / centre[:-1], np.repeat(damping[lat_rows::lat_rows], lat_rows)]
    )
    rows = rows.reshape(5, lat_devices, lat_rows).swapaxes(0, 1).astype(np.float32)
    return np.broadcast_to(rows[..., None], rows.shape + (levels,))


def in_vmem(array):
    return pltpu.with_memory_space_constraint(array, pltpu.VMEM)


def in_hbm(array):
    return pltpu.with_memory_space_constraint(array, pltpu.HBM)


def per_device(tendencies, bands, winds, tracers):
    fields, lat_rows, width, levels = tendencies.shape
    count = tracers.shape[0]
    lat_devices = lax.axis_size("lat")
    segments = lax.axis_size("lon")
    lat_place = lax.axis_index("lat")
    lon_place = lax.axis_index("lon")
    tendencies, winds, tracers = (a.transpose(0, 2, 1, 3) for a in (tendencies, winds, tracers))

    to_prior = [(i + 1, i) for i in range(lat_devices - 1)]
    to_next = [(i, i + 1) for i in range(lat_devices - 1)]
    west_ring = [((i + 1) % segments, i) for i in range(segments)]
    east_ring = [(i, (i + 1) % segments) for i in range(segments)]
    vmem = pl.BlockSpec(memory_space=pltpu.VMEM)
    smem = pl.BlockSpec(memory_space=pltpu.SMEM)
    hbm = pl.BlockSpec(memory_space=pltpu.HBM)
    params = pltpu.CompilerParams(vmem_limit_bytes=LIMIT)
    bf16 = jnp.bfloat16

    send = pl.pallas_call(
        pack_kernel,
        in_specs=[hbm],
        out_specs=hbm,
        out_shape=pltpu.HBM((segments, SEG, levels), bf16),
        scratch_shapes=[
            pltpu.VMEM(tendencies.shape, bf16),
            pltpu.VMEM((fields, width * lat_rows, levels), jnp.float32),
            pltpu.VMEM((segments, SEG, levels), bf16),
            pltpu.SemaphoreType.DMA((fields,)),
            pltpu.SemaphoreType.DMA((segments // lat_rows,)),
        ],
        compiler_params=params,
        name="pack",
    )(in_hbm(tendencies))
    with jax.named_scope("forth"):
        rows = lax.all_to_all(send, "lon", split_axis=0, concat_axis=0, tiled=True)

    factors = jnp.asarray(row_factors(lat_devices, lat_rows, levels))
    place = jnp.stack(
        [
            lat_place * lat_rows + lon_place % lat_rows,
            jnp.int32(lat_devices * lat_rows // 2),
            lat_place,
        ]
    )
    (p_one, p_two, q_one, q_two), waves, used = trig_tables(segments * width, segments)
    fold = np.where(used, np.where(waves == 0, 1.0, 2.0), 0.0) / (segments * width)
    with jax.named_scope("table"):
        table = (
            jnp.asarray(p_one)[:, None, :] * jnp.asarray(q_one)[None, :, :]
            + jnp.asarray(p_two)[:, None, :] * jnp.asarray(q_two)[None, :, :]
        )
        table = table.astype(bf16).reshape(segments * SEG, COEF)

    with jax.named_scope("edges"):
        high = jnp.concatenate(
            [tracers[:, 0].astype(bf16), winds[0:1, 0].astype(bf16), tendencies[0:1, 0]], axis=0
        )
        side = tracers[:, width - 1].astype(bf16)
        below = jnp.concatenate(
            [tracers[:, :, 0].astype(bf16), winds[1:2, :, 0].astype(bf16), tendencies[1:2, :, 0]], axis=0
        )
        top = tracers[:, :, lat_rows - 1].astype(bf16)
    with jax.named_scope("columns"):
        high = lax.ppermute(high, "lon", west_ring)
        side = lax.ppermute(side, "lon", east_ring)
    rows, table, factors, high, side, below, top = lax.optimization_barrier(
        (rows, table, factors, high, side, below, top)
    )

    low = pl.pallas_call(
        transform_kernel,
        in_specs=[smem, smem, vmem, vmem, vmem, hbm],
        out_specs=hbm,
        out_shape=pltpu.HBM((segments * SEG, levels), bf16),
        scratch_shapes=[
            pltpu.VMEM((segments * SEG, COEF), bf16),
            pltpu.VMEM((segments * SEG, levels), bf16),
            pltpu.SemaphoreType.DMA((CHUNKS,)),
            pltpu.SemaphoreType.DMA((CHUNKS,)),
        ],
        compiler_params=params,
        name="transform",
    )(
        place,
        bands,
        jnp.asarray(waves)[None],
        jnp.asarray(fold, jnp.float32)[None],
        in_vmem(rows.reshape(segments * SEG, levels)),
        in_hbm(table),
    )
    low, below, top = lax.optimization_barrier((low, below, top))
    with jax.named_scope("back"):
        low = lax.all_to_all(
            low.reshape(segments, SEG, levels), "lon", split_axis=0, concat_axis=0, tiled=True
        )
    with jax.named_scope("below"):
        below = lax.ppermute(below, "lat", to_prior)
    with jax.named_scope("top"):
        top = lax.ppermute(top, "lat", to_next)
    next_low = lax.ppermute(low[lat_rows], "lat", to_prior[: lat_devices // 2 - 1])

    filtered, edge = pl.pallas_call(
        filter_kernel,
        in_specs=[smem] + [vmem] * 4,
        out_specs=[vmem] * 2,
        out_shape=[
            jax.ShapeDtypeStruct(tendencies.shape, bf16),
            jax.ShapeDtypeStruct((lat_rows, levels), jnp.float32),
        ],
        scratch_shapes=[pltpu.VMEM((fields, SEG * lat_rows, levels), jnp.float32)],
        compiler_params=params,
        name="filter",
    )(place, in_vmem(low), in_vmem(factors), in_vmem(tendencies), in_vmem(high))

    blocks = width // COLS

    def whole(array):
        return pl.BlockSpec(array.shape, lambda i: (0,) * array.ndim)

    def part(size):
        return pl.BlockSpec((size, COLS, lat_rows, levels), lambda i: (0, blocks - 1 - i, 0, 0))

    advected = pl.pallas_call(
        advect_kernel,
        grid=(blocks,),
        in_specs=[
            smem,
            part(2),
            whole(factors),
            part(2),
            part(count),
            pl.BlockSpec(
                (count, 1, lat_rows, levels),
                lambda i: (0, jnp.maximum((blocks - 1 - i) * COLS - 1, 0), 0, 0),
            ),
            whole(edge),
            whole(high),
            whole(side),
            whole(below),
            whole(top),
            whole(next_low),
        ],
        out_specs=part(count),
        out_shape=jax.ShapeDtypeStruct(tracers.shape, jnp.float32),
        scratch_shapes=[
            pltpu.VMEM((SEG, levels), jnp.float32),
            pltpu.VMEM((count, lat_rows, levels), jnp.float32),
            pltpu.VMEM((count + 2, SEG, levels), jnp.float32),
            pltpu.VMEM((count, SEG, levels), jnp.float32),
        ],
        compiler_params=params,
        name="advect",
    )(
        place,
        in_hbm(filtered),
        factors,
        in_hbm(winds),
        in_hbm(tracers),
        in_hbm(tracers),
        edge,
        high,
        side,
        below,
        top,
        next_low,
    )
    return (filtered.transpose(0, 2, 1, 3), advected.transpose(0, 2, 1, 3))


def solution(mesh):
    return jax.shard_map(
        per_device,
        mesh=mesh,
        in_specs=(
            P(None, "lat", "lon", None),
            P(),
            P(None, "lat", "lon", None),
            P(None, "lat", "lon", None),
        ),
        out_specs=(P(None, "lat", "lon", None), P(None, "lat", "lon", None)),
        check_vma=False,
    )
```

```python
import math

import jax
import jax.numpy as jnp
import numpy as np
from jax import lax
from jax.experimental import pallas as pl
from jax.experimental.pallas import tpu as pltpu
from jax.sharding import PartitionSpec as P

HEMI = 720
KMAX = 180
COEF = 384
SEG = 48
LIMIT = 24 << 20
CHUNKS = 4
COLS = 9


def trig_tables(lon_count, segments):
    width = lon_count // segments
    k = np.zeros(COEF)
    k[: KMAX + 1] = np.arange(KMAX + 1)
    k[KMAX + 1 : 2 * KMAX + 1] = np.arange(1, KMAX + 1)
    is_cos = np.zeros(COEF, bool)
    is_cos[: KMAX + 1] = True
    used = np.arange(COEF) < 2 * KMAX + 1
    over_p = 2 * np.pi * np.outer(np.arange(segments) * width, k) / lon_count
    over_q = 2 * np.pi * np.outer(np.arange(SEG), k) / lon_count
    p_one = np.where(is_cos, np.cos(over_p), np.sin(over_p)) * used
    p_two = np.where(is_cos, -np.sin(over_p), np.cos(over_p)) * used
    tables = (p_one, p_two, np.cos(over_q), np.sin(over_q))
    return tuple(t.astype(np.float32) for t in tables), k.astype(np.int32), used


def pack_kernel(tend_ref, out_ref, tend, wide, rows, in_sems, out_sems):
    fields, width, lat_rows, levels = tend.shape
    pad = rows.shape[1] - width
    loads = [pltpu.make_async_copy(tend_ref.at[f], tend.at[f], in_sems.at[f]) for f in range(fields)]
    for load in loads:
        load.start()
    stores = []
    blocks = rows.shape[0] // lat_rows
    for f in reversed(range(blocks)):
        part = pl.ds(f * lat_rows, lat_rows)
        if f < fields:
            loads[f].wait()
            wide[f] = tend[f].astype(jnp.float32).reshape(width * lat_rows, levels)
            for r in range(lat_rows):
                row = wide[f, pl.ds(r, width, stride=lat_rows), :]
                rows[f * lat_rows + r, :width] = row.astype(jnp.bfloat16)
                rows[f * lat_rows + r, width:] = jnp.zeros((pad, levels), jnp.bfloat16)
        else:
            rows[part] = jnp.zeros((lat_rows,) + rows.shape[1:], jnp.bfloat16)
        store = pltpu.make_async_copy(rows.at[part], out_ref.at[part], out_sems.at[f])
        store.start()
        stores.append(store)
    for store in stores:
        store.wait()


def transform_kernel(rows_ref, weight_ref, table_ref, out_ref, rows, result, in_sems, out_sems):
    size = result.shape[0] // CHUNKS
    parts = [pl.ds(i * size, size) for i in range(CHUNKS)]
    loads = [
        pltpu.make_async_copy(rows_ref.at[part], rows.at[part], in_sems.at[i])
        for i, part in enumerate(parts)
    ]
    stores = [
        pltpu.make_async_copy(result.at[part], out_ref.at[part], out_sems.at[i])
        for i, part in enumerate(parts)
    ]
    for load in loads:
        load.start()
    spectrum = 0.0
    for load, part in zip(loads, parts):
        load.wait()
        spectrum += lax.dot_general(
            rows[part], table_ref[part], (((0,), (0,)), ((), ())), preferred_element_type=jnp.float32
        )
    weighted = (spectrum * weight_ref[...]).astype(jnp.bfloat16)
    for store, part in zip(stores, parts):
        result[part] = lax.dot_general(
            table_ref[part], weighted, (((1,), (1,)), ((), ())), preferred_element_type=jnp.float32
        ).astype(jnp.bfloat16)
        store.start()
    for store in stores:
        store.wait()


def filter_kernel(
    low_ref,
    factor_ref,
    tend_ref,
    wind_hbm,
    high_ref,
    filt_ref,
    courant_ref,
    wide_ref,
    filt,
    wind_ref,
    sems,
    wind_sems,
):
    fields, width, lat_rows, levels = tend_ref.shape
    loads = [pltpu.make_async_copy(wind_hbm.at[f], wind_ref.at[f], wind_sems.at[f]) for f in range(2)]
    for load in loads:
        load.start()
    size = width * lat_rows
    damp = jnp.broadcast_to(factor_ref[lax.axis_index("lat"), 0], (lat_rows, levels))
    stores = []
    for f in range(fields):
        for r in range(lat_rows):
            wide_ref[f, pl.ds(r, SEG, stride=lat_rows), :] = low_ref[f * lat_rows + r].astype(jnp.float32)
        low = wide_ref[f, :size].reshape(width, lat_rows, levels)
        value = (damp[None] * tend_ref[f].astype(jnp.float32) + low).astype(jnp.bfloat16)
        filt[f] = value
        stores.append(pltpu.make_async_copy(filt.at[f], filt_ref.at[f], sems.at[f]))
        stores[f].start()
        if f < 2:
            loads[f].wait()
            courant_ref[f, :width] = (0.5, 0.25)[f] * jnp.tanh(wind_ref[f] + value.astype(jnp.float32))
        if f == 0:
            last = high_ref.shape[0] - 1
            edge = damp * high_ref[last].astype(jnp.float32) + wide_ref[f, size : size + lat_rows]
            edge = edge.astype(jnp.bfloat16).astype(jnp.float32)
            courant_ref[f, width] = 0.5 * jnp.tanh(high_ref[last - 1].astype(jnp.float32) + edge)
    for store in stores:
        store.wait()


def advect_kernel(
    courant_ref,
    factor_ref,
    tracer_hbm,
    high_ref,
    side_ref,
    below_ref,
    top_ref,
    next_low_ref,
    out_hbm,
    tracer_ref,
    out_ref,
    north_ref,
    below_wide,
    top_wide,
    in_sems,
    out_sems,
):
    count, width, lat_rows, levels = tracer_ref.shape
    pieces = width // COLS
    loads = []
    stores = []
    for i in range(pieces):
        part = pl.ds(i * COLS, COLS)
        loads.append(
            pltpu.make_async_copy(tracer_hbm.at[:, part], tracer_ref.at[:, part], in_sems.at[i])
        )
        stores.append(pltpu.make_async_copy(out_ref.at[:, part], out_hbm.at[:, part], out_sems.at[i]))
    for load in reversed(loads):
        load.start()
    lat = lax.axis_index("lat")
    face, face_next, inverse = (
        jnp.broadcast_to(factor_ref[lat, i], (lat_rows, levels)) for i in (1, 2, 3)
    )
    sublane = lax.broadcasted_iota(jnp.int32, (lat_rows, levels), 0)
    is_first = sublane == 0
    is_last = sublane == lat_rows - 1
    below_wide[:, :width] = below_ref[...].astype(jnp.float32)
    top_wide[:, :width] = top_ref[...].astype(jnp.float32)
    filt = factor_ref[lat, 4, 0:1] * below_wide[count + 1, :width]
    filt = (filt + next_low_ref[:width].astype(jnp.float32)).astype(jnp.bfloat16)
    north_ref[:width] = 0.25 * jnp.tanh(below_wide[count, :width] + filt.astype(jnp.float32))
    loads[pieces - 1].wait()
    east = courant_ref[0, width]
    flux = [
        jnp.maximum(east, 0.0) * tracer_ref[q, width - 1]
        + jnp.minimum(east, 0.0) * high_ref[q].astype(jnp.float32)
        for q in range(count)
    ]
    for piece in reversed(range(pieces)):
        if piece > 0:
            loads[piece - 1].wait()
        for column in reversed(range(piece * COLS, (piece + 1) * COLS)):
            east = courant_ref[0, column]
            north = courant_ref[1, column]
            north_next = jnp.where(
                is_last, north_ref[column : column + 1], pltpu.roll(north, lat_rows - 1, 0)
            )
            west_plus = jnp.maximum(east, 0.0)
            west_minus = jnp.minimum(east, 0.0)
            pole_plus = face * jnp.maximum(north, 0.0)
            pole_minus = face * jnp.minimum(north, 0.0)
            next_plus = face_next * jnp.maximum(north_next, 0.0)
            next_minus = face_next * jnp.minimum(north_next, 0.0)
            for q in range(count):
                here = tracer_ref[q, column]
                if column > 0:
                    west = tracer_ref[q, column - 1]
                else:
                    west = side_ref[q].astype(jnp.float32)
                prior = jnp.where(
                    is_first, top_wide[q, column : column + 1], pltpu.roll(here, 1, 0)
                )
                after = jnp.where(
                    is_last, below_wide[q, column : column + 1], pltpu.roll(here, lat_rows - 1, 0)
                )
                f_west = west_plus * west + west_minus * here
                g_pole = pole_plus * prior + pole_minus * here
                g_next = next_plus * here + next_minus * after
                out_ref[q, column] = here - (flux[q] - f_west) - (g_next - g_pole) * inverse
                flux[q] = f_west
        stores[piece].start()
    for store in stores:
        store.wait()


def row_factors(lat_devices, lat_rows):
    ids = np.arange(lat_devices * lat_rows + 1)
    half = lat_devices * lat_rows // 2
    damping = np.where(ids < half, 0.25 + 0.5 * (ids + 0.5) / half, 1.0)
    grid_row = ids + HEMI // 2 - half
    face = np.sin(math.pi * grid_row / (2.0 * HEMI))
    centre = np.sin(math.pi * (grid_row + 0.5) / (2.0 * HEMI))
    rows = np.stack(
        [damping[:-1], face[:-1], face[1:], 1.0 / centre[:-1], np.repeat(damping[lat_rows::lat_rows], lat_rows)]
    )
    rows = rows.reshape(5, lat_devices, lat_rows).swapaxes(0, 1).astype(np.float32)
    return rows[..., None]


def in_vmem(array):
    return pltpu.with_memory_space_constraint(array, pltpu.VMEM)


def in_hbm(array):
    return pltpu.with_memory_space_constraint(array, pltpu.HBM)


def per_device(tendencies, bands, winds, tracers):
    fields, lat_rows, width, levels = tendencies.shape
    count = tracers.shape[0]
    lat_devices = lax.axis_size("lat")
    segments = lax.axis_size("lon")
    lat_place = lax.axis_index("lat")
    lon_place = lax.axis_index("lon")
    tendencies, winds, tracers = (a.transpose(0, 2, 1, 3) for a in (tendencies, winds, tracers))

    to_prior = [(i + 1, i) for i in range(lat_devices - 1)]
    to_next = [(i, i + 1) for i in range(lat_devices - 1)]
    west_ring = [((i + 1) % segments, i) for i in range(segments)]
    east_ring = [(i, (i + 1) % segments) for i in range(segments)]
    vmem = pl.BlockSpec(memory_space=pltpu.VMEM)
    hbm = pl.BlockSpec(memory_space=pltpu.HBM)
    params = pltpu.CompilerParams(vmem_limit_bytes=LIMIT)
    bf16 = jnp.bfloat16

    send = pl.pallas_call(
        pack_kernel,
        in_specs=[hbm],
        out_specs=hbm,
        out_shape=pltpu.HBM((segments, SEG, levels), bf16),
        scratch_shapes=[
            pltpu.VMEM(tendencies.shape, bf16),
            pltpu.VMEM((fields, width * lat_rows, levels), jnp.float32),
            pltpu.VMEM((segments, SEG, levels), bf16),
            pltpu.SemaphoreType.DMA((fields,)),
            pltpu.SemaphoreType.DMA((segments // lat_rows,)),
        ],
        compiler_params=params,
        name="pack",
    )(in_hbm(tendencies))
    with jax.named_scope("forth"):
        rows = lax.all_to_all(send, "lon", split_axis=0, concat_axis=0, tiled=True)

    factors = jnp.asarray(row_factors(lat_devices, lat_rows))
    (p_one, p_two, q_one, q_two), waves, used = trig_tables(segments * width, segments)
    row = lat_place * lat_rows + lon_place % lat_rows
    half = lat_devices * lat_rows // 2
    damping = 0.25 + 0.5 * (row.astype(jnp.float32) + 0.5) / half
    damping = jnp.where(row < half, damping, 1.0)
    fold = np.where(used, np.where(waves == 0, 1.0, 2.0), 0.0) / (segments * width)
    weight = (1.0 - damping) * jnp.asarray(fold, jnp.float32)[None]
    weight = jnp.where(jnp.asarray(waves)[None] <= bands[row], weight, 0.0)
    with jax.named_scope("table"):
        table = (
            jnp.asarray(p_one)[:, None, :] * jnp.asarray(q_one)[None, :, :]
            + jnp.asarray(p_two)[:, None, :] * jnp.asarray(q_two)[None, :, :]
        )
        table = table.astype(bf16).reshape(segments * SEG, COEF)

    with jax.named_scope("edges"):
        high = jnp.concatenate(
            [tracers[:, 0].astype(bf16), winds[0:1, 0].astype(bf16), tendencies[0:1, 0]], axis=0
        )
        side = tracers[:, width - 1].astype(bf16)
        below = jnp.concatenate(
            [tracers[:, :, 0].astype(bf16), winds[1:2, :, 0].astype(bf16), tendencies[1:2, :, 0]], axis=0
        )
        top = tracers[:, :, lat_rows - 1].astype(bf16)
    with jax.named_scope("columns"):
        high = lax.ppermute(high, "lon", west_ring)
        side = lax.ppermute(side, "lon", east_ring)
    rows, table, weight, factors, high, side, below, top = lax.optimization_barrier(
        (rows, table, weight, factors, high, side, below, top)
    )

    low = pl.pallas_call(
        transform_kernel,
        in_specs=[hbm, vmem, vmem],
        out_specs=hbm,
        out_shape=pltpu.HBM((segments * SEG, levels), bf16),
        scratch_shapes=[
            pltpu.VMEM((segments * SEG, levels), bf16),
            pltpu.VMEM((segments * SEG, levels), bf16),
            pltpu.SemaphoreType.DMA((CHUNKS,)),
            pltpu.SemaphoreType.DMA((CHUNKS,)),
        ],
        compiler_params=params,
        name="transform",
    )(in_hbm(rows.reshape(segments * SEG, levels)), in_vmem(weight), in_vmem(table))
    low, below, top = lax.optimization_barrier((low, below, top))
    with jax.named_scope("back"):
        low = lax.all_to_all(
            low.reshape(segments, SEG, levels), "lon", split_axis=0, concat_axis=0, tiled=True
        )
    with jax.named_scope("below"):
        below = lax.ppermute(below, "lat", to_prior)
    with jax.named_scope("top"):
        top = lax.ppermute(top, "lat", to_next)
    next_low = lax.ppermute(low[lat_rows], "lat", to_prior[: lat_devices // 2 - 1])

    filtered, courant = pl.pallas_call(
        filter_kernel,
        in_specs=[vmem, vmem, vmem, hbm, vmem],
        out_specs=[hbm, vmem],
        out_shape=[
            pltpu.HBM(tendencies.shape, bf16),
            pltpu.VMEM((2, width + 1, lat_rows, levels), jnp.float32),
        ],
        scratch_shapes=[
            pltpu.VMEM((fields, SEG * lat_rows, levels), jnp.float32),
            pltpu.VMEM(tendencies.shape, bf16),
            pltpu.VMEM(winds.shape, jnp.float32),
            pltpu.SemaphoreType.DMA((fields,)),
            pltpu.SemaphoreType.DMA((2,)),
        ],
        compiler_params=params,
        name="filter",
    )(in_vmem(low), in_vmem(factors), in_vmem(tendencies), in_hbm(winds), in_vmem(high))
    advected = pl.pallas_call(
        advect_kernel,
        in_specs=[vmem, vmem, hbm] + [vmem] * 5,
        out_specs=hbm,
        out_shape=pltpu.HBM(tracers.shape, jnp.float32),
        scratch_shapes=[
            pltpu.VMEM(tracers.shape, jnp.float32),
            pltpu.VMEM(tracers.shape, jnp.float32),
            pltpu.VMEM((SEG, levels), jnp.float32),
            pltpu.VMEM((count + 2, SEG, levels), jnp.float32),
            pltpu.VMEM((count, SEG, levels), jnp.float32),
            pltpu.SemaphoreType.DMA((width // COLS,)),
            pltpu.SemaphoreType.DMA((width // COLS,)),
        ],
        compiler_params=params,
        name="advect",
    )(
        courant,
        in_vmem(factors),
        in_hbm(tracers),
        in_vmem(high),
        in_vmem(side),
        in_vmem(below),
        in_vmem(top),
        in_vmem(next_low),
    )
    return (filtered.transpose(0, 2, 1, 3), advected.transpose(0, 2, 1, 3))


def solution(mesh):
    return jax.shard_map(
        per_device,
        mesh=mesh,
        in_specs=(
            P(None, "lat", "lon", None),
            P(),
            P(None, "lat", "lon", None),
            P(None, "lat", "lon", None),
        ),
        out_specs=(P(None, "lat", "lon", None), P(None, "lat", "lon", None)),
        check_vma=False,
    )
```

```python
import math

import jax
import jax.numpy as jnp
import numpy as np
from jax import lax
from jax.experimental import pallas as pl
from jax.experimental.pallas import tpu as pltpu
from jax.sharding import PartitionSpec as P

HEMI = 720
KMAX = 180
COEF = 384
SEG = 48
HEAD = 40
QUARTER = 32
MAIN = 96
LIMIT = 24 << 20
LOADS = 5
CHUNKS = 4
COLS = 9


def trig_tables(lon_count, segments):
    width = lon_count // segments
    k = np.zeros(COEF)
    k[: KMAX + 1] = np.arange(KMAX + 1)
    k[KMAX + 1 : 2 * KMAX + 1] = np.arange(1, KMAX + 1)
    is_cos = np.zeros(COEF, bool)
    is_cos[: KMAX + 1] = True
    used = np.arange(COEF) < 2 * KMAX + 1
    over_p = 2 * np.pi * np.outer(np.arange(segments) * width, k) / lon_count
    over_q = 2 * np.pi * np.outer(np.arange(SEG), k) / lon_count
    p_one = np.where(is_cos, np.cos(over_p), np.sin(over_p)) * used
    p_two = np.where(is_cos, -np.sin(over_p), np.cos(over_p)) * used
    tables = (p_one, p_two, np.cos(over_q), np.sin(over_q))
    return tuple(t.astype(np.float32) for t in tables), k.astype(np.int32), used


def squeeze(head, tail):
    lane = lax.broadcasted_iota(jnp.int32, tail.shape, tail.ndim - 1)
    size = tail.shape[-2]
    groups = [
        jnp.where(
            lane < MAIN,
            head[..., i * size : (i + 1) * size, :],
            pltpu.roll(tail, MAIN - i * QUARTER, tail.ndim - 1),
        )
        for i in range(MAIN // QUARTER)
    ]
    return jnp.concatenate(groups + [head[..., MAIN // QUARTER * size :, :]], axis=-2)


def tail_of(head):
    size = SEG - HEAD
    moved = [
        pltpu.roll(head[..., i * size : (i + 1) * size, :], (i + 1) * QUARTER, head.ndim - 1)
        for i in range(MAIN // QUARTER)
    ]
    lane = lax.broadcasted_iota(jnp.int32, moved[0].shape, head.ndim - 1)
    return jnp.where(lane < QUARTER, moved[0], jnp.where(lane < 2 * QUARTER, moved[1], moved[2]))


def expand(head):
    return jnp.concatenate([head, tail_of(head)], axis=-2)


def with_rest(row, rest, f):
    lane = lax.broadcasted_iota(jnp.int32, row.shape, row.ndim - 1)
    return jnp.where(lane < MAIN, row, pltpu.roll(rest, MAIN - f * QUARTER, row.ndim - 1))


def pack_kernel(tend_ref, out_ref, tend, wide, rows, in_sems, out_sems):
    fields, width, lat_rows, levels = tend.shape
    size = width * lat_rows
    loads = [pltpu.make_async_copy(tend_ref.at[f], tend.at[f], in_sems.at[f]) for f in range(fields)]
    for load in loads:
        load.start()
    stores = []

    def send(block):
        part = pl.ds(block * lat_rows, lat_rows)
        store = pltpu.make_async_copy(rows.at[part], out_ref.at[part], out_sems.at[block])
        store.start()
        stores.append(store)

    for f in range(fields):
        wide[f, size:] = jnp.zeros((SEG * lat_rows - size, levels), jnp.float32)
    for f in range(fields):
        loads[f].wait()
        wide[f, :size] = tend[f].astype(jnp.float32).reshape(size, levels)
        for r in range(lat_rows):
            row = wide[f, pl.ds(r, SEG, stride=lat_rows), :]
            rows[f * lat_rows + r] = squeeze(row[:HEAD], row[HEAD:]).astype(jnp.bfloat16)
        send(f)
    lane = lax.broadcasted_iota(jnp.int32, (SEG, levels), 1)
    for r in range(lat_rows):
        moved = [
            pltpu.roll(wide[f, pl.ds(r, SEG, stride=lat_rows), :], (f + 1) * QUARTER, 1)
            for f in range(fields)
        ]
        row = jnp.where(lane < QUARTER, moved[0], jnp.where(lane < 2 * QUARTER, moved[1], moved[2]))
        rows[fields * lat_rows + r] = squeeze(row[:HEAD], row[HEAD:]).astype(jnp.bfloat16)
    send(fields)
    for store in stores:
        store.wait()


def transform_kernel(
    rows_ref, weight_ref, head_ref, tail_ref, out_ref, rows, result, in_sems, out_sems
):
    total, levels = rows.shape
    tails = SEG - HEAD
    segments = total // HEAD
    piece = total // LOADS
    loads = [
        pltpu.make_async_copy(
            rows_ref.at[pl.ds(i * piece, piece)], rows.at[pl.ds(i * piece, piece)], in_sems.at[i]
        )
        for i in range(LOADS)
    ]
    for load in loads:
        load.start()
    forward = (((0,), (0,)), ((), ()))
    back = (((1,), (1,)), ((), ()))
    spectrum = 0.0
    for i, load in enumerate(loads):
        load.wait()
        part = pl.ds(i * piece, piece)
        spectrum += lax.dot_general(
            rows[part], head_ref[part], forward, preferred_element_type=jnp.float32
        )
    tail = tail_of(rows[...].astype(jnp.float32).reshape(segments, HEAD, levels))
    tail = tail.reshape(segments * tails, levels).astype(jnp.bfloat16)
    spectrum += lax.dot_general(tail, tail_ref[...], forward, preferred_element_type=jnp.float32)
    weighted = (spectrum * weight_ref[...]).astype(jnp.bfloat16)
    tail = lax.dot_general(tail_ref[...], weighted, back, preferred_element_type=jnp.float32)
    tail = tail.reshape(segments, tails, levels)
    count = segments // CHUNKS
    stores = []
    for i in range(CHUNKS):
        part = pl.ds(i * count * HEAD, count * HEAD)
        head = lax.dot_general(head_ref[part], weighted, back, preferred_element_type=jnp.float32)
        head = squeeze(head.reshape(count, HEAD, levels), tail[i * count : (i + 1) * count])
        result[part] = head.reshape(count * HEAD, levels).astype(jnp.bfloat16)
        stores.append(pltpu.make_async_copy(result.at[part], out_ref.at[part], out_sems.at[i]))
        stores[i].start()
    for store in stores:
        store.wait()


def filter_kernel(
    low_ref,
    factor_ref,
    tend_ref,
    wind_hbm,
    high_ref,
    filt_ref,
    courant_ref,
    wide_ref,
    rest_ref,
    filt,
    wind_ref,
    sems,
    wind_sems,
):
    fields, width, lat_rows, levels = tend_ref.shape
    loads = [pltpu.make_async_copy(wind_hbm.at[f], wind_ref.at[f], wind_sems.at[f]) for f in range(2)]
    for load in loads:
        load.start()
    size = width * lat_rows
    damp = jnp.broadcast_to(factor_ref[lax.axis_index("lat"), 0], (lat_rows, levels))
    stores = []
    for r in range(lat_rows):
        rest_ref[r] = expand(low_ref[fields * lat_rows + r].astype(jnp.float32))
    for f in range(fields):
        for r in range(lat_rows):
            row = expand(low_ref[f * lat_rows + r].astype(jnp.float32))
            wide_ref[f, pl.ds(r, SEG, stride=lat_rows), :] = with_rest(row, rest_ref[r], f)
        low = wide_ref[f, :size].reshape(width, lat_rows, levels)
        value = (damp[None] * tend_ref[f].astype(jnp.float32) + low).astype(jnp.bfloat16)
        filt[f] = value
        stores.append(pltpu.make_async_copy(filt.at[f], filt_ref.at[f], sems.at[f]))
        stores[f].start()
        if f < 2:
            loads[f].wait()
            courant_ref[f, :width] = (0.5, 0.25)[f] * jnp.tanh(wind_ref[f] + value.astype(jnp.float32))
        if f == 0:
            last = high_ref.shape[0] - 1
            edge = damp * high_ref[last].astype(jnp.float32) + wide_ref[f, size : size + lat_rows]
            edge = edge.astype(jnp.bfloat16).astype(jnp.float32)
            courant_ref[f, width] = 0.5 * jnp.tanh(high_ref[last - 1].astype(jnp.float32) + edge)
    for store in stores:
        store.wait()


def advect_kernel(
    courant_ref,
    factor_ref,
    tracer_hbm,
    high_ref,
    side_ref,
    below_ref,
    top_ref,
    next_low_ref,
    out_hbm,
    tracer_ref,
    out_ref,
    north_ref,
    below_wide,
    top_wide,
    in_sems,
    out_sems,
):
    count, width, lat_rows, levels = tracer_ref.shape
    pieces = width // COLS
    loads = []
    stores = []
    for i in range(pieces):
        part = pl.ds(i * COLS, COLS)
        loads.append(
            pltpu.make_async_copy(tracer_hbm.at[:, part], tracer_ref.at[:, part], in_sems.at[i])
        )
        stores.append(pltpu.make_async_copy(out_ref.at[:, part], out_hbm.at[:, part], out_sems.at[i]))
    for load in reversed(loads):
        load.start()
    lat = lax.axis_index("lat")
    face, face_next, inverse = (
        jnp.broadcast_to(factor_ref[lat, i], (lat_rows, levels)) for i in (1, 2, 3)
    )
    sublane = lax.broadcasted_iota(jnp.int32, (lat_rows, levels), 0)
    is_first = sublane == 0
    is_last = sublane == lat_rows - 1
    below_wide[:, :width] = below_ref[...].astype(jnp.float32)
    top_wide[:, :width] = top_ref[...].astype(jnp.float32)
    filt = factor_ref[lat, 4, 0:1] * below_wide[count + 1, :width]
    row, rest = (expand(next_low_ref[i].astype(jnp.float32)) for i in range(2))
    filt = (filt + with_rest(row, rest, 1)[:width]).astype(jnp.bfloat16)
    north_ref[:width] = 0.25 * jnp.tanh(below_wide[count, :width] + filt.astype(jnp.float32))
    loads[pieces - 1].wait()
    east = courant_ref[0, width]
    flux = [
        jnp.maximum(east, 0.0) * tracer_ref[q, width - 1]
        + jnp.minimum(east, 0.0) * high_ref[q].astype(jnp.float32)
        for q in range(count)
    ]
    for piece in reversed(range(pieces)):
        if piece > 0:
            loads[piece - 1].wait()
        for column in reversed(range(piece * COLS, (piece + 1) * COLS)):
            east = courant_ref[0, column]
            north = courant_ref[1, column]
            north_next = jnp.where(
                is_last, north_ref[column : column + 1], pltpu.roll(north, lat_rows - 1, 0)
            )
            west_plus = jnp.maximum(east, 0.0)
            west_minus = jnp.minimum(east, 0.0)
            pole_plus = face * jnp.maximum(north, 0.0)
            pole_minus = face * jnp.minimum(north, 0.0)
            next_plus = face_next * jnp.maximum(north_next, 0.0)
            next_minus = face_next * jnp.minimum(north_next, 0.0)
            for q in range(count):
                here = tracer_ref[q, column]
                if column > 0:
                    west = tracer_ref[q, column - 1]
                else:
                    west = side_ref[q].astype(jnp.float32)
                prior = jnp.where(
                    is_first, top_wide[q, column : column + 1], pltpu.roll(here, 1, 0)
                )
                after = jnp.where(
                    is_last, below_wide[q, column : column + 1], pltpu.roll(here, lat_rows - 1, 0)
                )
                f_west = west_plus * west + west_minus * here
                g_pole = pole_plus * prior + pole_minus * here
                g_next = next_plus * here + next_minus * after
                out_ref[q, column] = here - (flux[q] - f_west) - (g_next - g_pole) * inverse
                flux[q] = f_west
        stores[piece].start()
    for store in stores:
        store.wait()


def row_factors(lat_devices, lat_rows):
    ids = np.arange(lat_devices * lat_rows + 1)
    half = lat_devices * lat_rows // 2
    damping = np.where(ids < half, 0.25 + 0.5 * (ids + 0.5) / half, 1.0)
    grid_row = ids + HEMI // 2 - half
    face = np.sin(math.pi * grid_row / (2.0 * HEMI))
    centre = np.sin(math.pi * (grid_row + 0.5) / (2.0 * HEMI))
    rows = np.stack(
        [damping[:-1], face[:-1], face[1:], 1.0 / centre[:-1], np.repeat(damping[lat_rows::lat_rows], lat_rows)]
    )
    rows = rows.reshape(5, lat_devices, lat_rows).swapaxes(0, 1).astype(np.float32)
    return rows[..., None]


def in_vmem(array):
    return pltpu.with_memory_space_constraint(array, pltpu.VMEM)


def in_hbm(array):
    return pltpu.with_memory_space_constraint(array, pltpu.HBM)


def per_device(tendencies, bands, winds, tracers):
    fields, lat_rows, width, levels = tendencies.shape
    count = tracers.shape[0]
    lat_devices = lax.axis_size("lat")
    segments = lax.axis_size("lon")
    lat_place = lax.axis_index("lat")
    lon_place = lax.axis_index("lon")
    tendencies, winds, tracers = (a.transpose(0, 2, 1, 3) for a in (tendencies, winds, tracers))

    to_prior = [(i + 1, i) for i in range(lat_devices - 1)]
    to_next = [(i, i + 1) for i in range(lat_devices - 1)]
    west_ring = [((i + 1) % segments, i) for i in range(segments)]
    east_ring = [(i, (i + 1) % segments) for i in range(segments)]
    vmem = pl.BlockSpec(memory_space=pltpu.VMEM)
    hbm = pl.BlockSpec(memory_space=pltpu.HBM)
    params = pltpu.CompilerParams(vmem_limit_bytes=LIMIT)
    bf16 = jnp.bfloat16

    send = pl.pallas_call(
        pack_kernel,
        in_specs=[hbm],
        out_specs=hbm,
        out_shape=pltpu.HBM((segments, HEAD, levels), bf16),
        scratch_shapes=[
            pltpu.VMEM(tendencies.shape, bf16),
            pltpu.VMEM((fields, SEG * lat_rows, levels), jnp.float32),
            pltpu.VMEM((segments, HEAD, levels), bf16),
            pltpu.SemaphoreType.DMA((fields,)),
            pltpu.SemaphoreType.DMA((segments // lat_rows,)),
        ],
        compiler_params=params,
        name="pack",
    )(in_hbm(tendencies))
    with jax.named_scope("forth"):
        rows = lax.all_to_all(send, "lon", split_axis=0, concat_axis=0, tiled=True)

    factors = jnp.asarray(row_factors(lat_devices, lat_rows))
    (p_one, p_two, q_one, q_two), waves, used = trig_tables(segments * width, segments)
    row = lat_place * lat_rows + lon_place % lat_rows
    half = lat_devices * lat_rows // 2
    damping = 0.25 + 0.5 * (row.astype(jnp.float32) + 0.5) / half
    damping = jnp.where(row < half, damping, 1.0)
    fold = np.where(used, np.where(waves == 0, 1.0, 2.0), 0.0) / (segments * width)
    weight = (1.0 - damping) * jnp.asarray(fold, jnp.float32)[None]
    weight = jnp.where(jnp.asarray(waves)[None] <= bands[row], weight, 0.0)
    with jax.named_scope("table"):
        head_table, tail_table = (
            (
                jnp.asarray(p_one)[:, None, :] * jnp.asarray(q_one[part])[None, :, :]
                + jnp.asarray(p_two)[:, None, :] * jnp.asarray(q_two[part])[None, :, :]
            )
            .astype(bf16)
            .reshape(-1, COEF)
            for part in (slice(0, HEAD), slice(HEAD, SEG))
        )

    with jax.named_scope("edges"):
        high = jnp.concatenate(
            [tracers[:, 0].astype(bf16), winds[0:1, 0].astype(bf16), tendencies[0:1, 0]], axis=0
        )
        side = tracers[:, width - 1].astype(bf16)
        below = jnp.concatenate(
            [tracers[:, :, 0].astype(bf16), winds[1:2, :, 0].astype(bf16), tendencies[1:2, :, 0]], axis=0
        )
        top = tracers[:, :, lat_rows - 1].astype(bf16)
    with jax.named_scope("columns"):
        high = lax.ppermute(high, "lon", west_ring)
        side = lax.ppermute(side, "lon", east_ring)
    rows, head_table, tail_table, weight, high, side, below, top = lax.optimization_barrier(
        (rows, head_table, tail_table, weight, high, side, below, top)
    )

    low = pl.pallas_call(
        transform_kernel,
        in_specs=[hbm, vmem, vmem, vmem],
        out_specs=hbm,
        out_shape=pltpu.HBM((segments * HEAD, levels), bf16),
        scratch_shapes=[
            pltpu.VMEM((segments * HEAD, levels), bf16),
            pltpu.VMEM((segments * HEAD, levels), bf16),
            pltpu.SemaphoreType.DMA((LOADS,)),
            pltpu.SemaphoreType.DMA((CHUNKS,)),
        ],
        compiler_params=params,
        name="transform",
    )(
        in_hbm(rows.reshape(segments * HEAD, levels)),
        in_vmem(weight),
        in_vmem(head_table),
        in_vmem(tail_table),
    )
    low, below, top = lax.optimization_barrier((low, below, top))
    with jax.named_scope("back"):
        low = lax.all_to_all(
            low.reshape(segments, HEAD, levels), "lon", split_axis=0, concat_axis=0, tiled=True
        )
    with jax.named_scope("below"):
        below = lax.ppermute(below, "lat", to_prior)
    with jax.named_scope("top"):
        top = lax.ppermute(top, "lat", to_next)
    next_low = jnp.stack([low[lat_rows], low[fields * lat_rows]])
    next_low = lax.ppermute(next_low, "lat", to_prior[: lat_devices // 2 - 1])

    filtered, courant = pl.pallas_call(
        filter_kernel,
        in_specs=[vmem, vmem, vmem, hbm, vmem],
        out_specs=[hbm, vmem],
        out_shape=[
            pltpu.HBM(tendencies.shape, bf16),
            pltpu.VMEM((2, width + 1, lat_rows, levels), jnp.float32),
        ],
        scratch_shapes=[
            pltpu.VMEM((fields, SEG * lat_rows, levels), jnp.float32),
            pltpu.VMEM((lat_rows, SEG, levels), jnp.float32),
            pltpu.VMEM(tendencies.shape, bf16),
            pltpu.VMEM(winds.shape, jnp.float32),
            pltpu.SemaphoreType.DMA((fields,)),
            pltpu.SemaphoreType.DMA((2,)),
        ],
        compiler_params=params,
        name="filter",
    )(in_vmem(low), in_vmem(factors), in_vmem(tendencies), in_hbm(winds), in_vmem(high))
    advected = pl.pallas_call(
        advect_kernel,
        in_specs=[vmem, vmem, hbm] + [vmem] * 5,
        out_specs=hbm,
        out_shape=pltpu.HBM(tracers.shape, jnp.float32),
        scratch_shapes=[
            pltpu.VMEM(tracers.shape, jnp.float32),
            pltpu.VMEM(tracers.shape, jnp.float32),
            pltpu.VMEM((SEG, levels), jnp.float32),
            pltpu.VMEM((count + 2, SEG, levels), jnp.float32),
            pltpu.VMEM((count, SEG, levels), jnp.float32),
            pltpu.SemaphoreType.DMA((width // COLS,)),
            pltpu.SemaphoreType.DMA((width // COLS,)),
        ],
        compiler_params=params,
        name="advect",
    )(
        courant,
        in_vmem(factors),
        in_hbm(tracers),
        in_vmem(high),
        in_vmem(side),
        in_vmem(below),
        in_vmem(top),
        in_vmem(next_low),
    )
    return (filtered.transpose(0, 2, 1, 3), advected.transpose(0, 2, 1, 3))


def solution(mesh):
    return jax.shard_map(
        per_device,
        mesh=mesh,
        in_specs=(
            P(None, "lat", "lon", None),
            P(),
            P(None, "lat", "lon", None),
            P(None, "lat", "lon", None),
        ),
        out_specs=(P(None, "lat", "lon", None), P(None, "lat", "lon", None)),
        check_vma=False,
    )
```

```python
import functools
import math

import jax
import jax.numpy as jnp
import numpy as np
from jax import lax
from jax.experimental import pallas as pl
from jax.experimental.pallas import tpu as pltpu
from jax.sharding import PartitionSpec as P

HEMI = 720
KMAX = 180
COEF = 384
SEG = 48
HEAD = 40
QUARTER = 32
MAIN = 96
LIMIT = 24 << 20
LOADS = 5
CHUNKS = 4
COLS = 9


def trig_tables(lon_count, segments):
    width = lon_count // segments
    k = np.zeros(COEF)
    k[: KMAX + 1] = np.arange(KMAX + 1)
    k[KMAX + 1 : 2 * KMAX + 1] = np.arange(1, KMAX + 1)
    is_cos = np.zeros(COEF, bool)
    is_cos[: KMAX + 1] = True
    used = np.arange(COEF) < 2 * KMAX + 1
    over_p = 2 * np.pi * np.outer(np.arange(segments) * width, k) / lon_count
    over_q = 2 * np.pi * np.outer(np.arange(SEG), k) / lon_count
    p_one = np.where(is_cos, np.cos(over_p), np.sin(over_p)) * used
    p_two = np.where(is_cos, -np.sin(over_p), np.cos(over_p)) * used
    tables = (p_one, p_two, np.cos(over_q), np.sin(over_q))
    return tuple(t.astype(np.float32) for t in tables), k.astype(np.int32), used


def squeeze(head, tail):
    lane = lax.broadcasted_iota(jnp.int32, tail.shape, tail.ndim - 1)
    size = tail.shape[-2]
    groups = [
        jnp.where(
            lane < MAIN,
            head[..., i * size : (i + 1) * size, :],
            pltpu.roll(tail, MAIN - i * QUARTER, tail.ndim - 1),
        )
        for i in range(MAIN // QUARTER)
    ]
    return jnp.concatenate(groups + [head[..., MAIN // QUARTER * size :, :]], axis=-2)


def tail_of(head):
    size = SEG - HEAD
    moved = [
        pltpu.roll(head[..., i * size : (i + 1) * size, :], (i + 1) * QUARTER, head.ndim - 1)
        for i in range(MAIN // QUARTER)
    ]
    lane = lax.broadcasted_iota(jnp.int32, moved[0].shape, head.ndim - 1)
    return jnp.where(lane < QUARTER, moved[0], jnp.where(lane < 2 * QUARTER, moved[1], moved[2]))


def expand(head):
    return jnp.concatenate([head, tail_of(head)], axis=-2)


def with_rest(row, rest, f):
    lane = lax.broadcasted_iota(jnp.int32, row.shape, row.ndim - 1)
    return jnp.where(lane < MAIN, row, pltpu.roll(rest, MAIN - f * QUARTER, row.ndim - 1))


def pack_kernel(tend_ref, out_ref, tend, wide, rows, in_sems, out_sems):
    fields, width, lat_rows, levels = tend.shape
    size = width * lat_rows
    loads = [pltpu.make_async_copy(tend_ref.at[f], tend.at[f], in_sems.at[f]) for f in range(fields)]
    for load in loads:
        load.start()
    stores = []

    def send(block):
        part = pl.ds(block * lat_rows, lat_rows)
        store = pltpu.make_async_copy(rows.at[part], out_ref.at[part], out_sems.at[block])
        store.start()
        stores.append(store)

    for f in range(fields):
        wide[f, size:] = jnp.zeros((SEG * lat_rows - size, levels), jnp.float32)
    for f in range(fields):
        loads[f].wait()
        wide[f, :size] = tend[f].astype(jnp.float32).reshape(size, levels)
        for r in range(lat_rows):
            row = wide[f, pl.ds(r, SEG, stride=lat_rows), :]
            rows[f * lat_rows + r] = squeeze(row[:HEAD], row[HEAD:]).astype(jnp.bfloat16)
        send(f)
    lane = lax.broadcasted_iota(jnp.int32, (SEG, levels), 1)
    for r in range(lat_rows):
        moved = [
            pltpu.roll(wide[f, pl.ds(r, SEG, stride=lat_rows), :], (f + 1) * QUARTER, 1)
            for f in range(fields)
        ]
        row = jnp.where(lane < QUARTER, moved[0], jnp.where(lane < 2 * QUARTER, moved[1], moved[2]))
        rows[fields * lat_rows + r] = squeeze(row[:HEAD], row[HEAD:]).astype(jnp.bfloat16)
    send(fields)
    for store in stores:
        store.wait()


def transform_kernel(
    rows_ref, weight_ref, head_ref, tail_ref, out_ref, rows, result, in_sems, out_sems
):
    total, levels = rows.shape
    tails = SEG - HEAD
    segments = total // HEAD
    piece = total // LOADS
    loads = [
        pltpu.make_async_copy(
            rows_ref.at[pl.ds(i * piece, piece)], rows.at[pl.ds(i * piece, piece)], in_sems.at[i]
        )
        for i in range(LOADS)
    ]
    for load in loads:
        load.start()
    forward = (((0,), (0,)), ((), ()))
    back = (((1,), (1,)), ((), ()))
    spectrum = 0.0
    for i, load in enumerate(loads):
        load.wait()
        part = pl.ds(i * piece, piece)
        spectrum += lax.dot_general(
            rows[part], head_ref[part], forward, preferred_element_type=jnp.float32
        )
    tail = tail_of(rows[...].astype(jnp.float32).reshape(segments, HEAD, levels))
    tail = tail.reshape(segments * tails, levels).astype(jnp.bfloat16)
    spectrum += lax.dot_general(tail, tail_ref[...], forward, preferred_element_type=jnp.float32)
    weighted = (spectrum * weight_ref[...]).astype(jnp.bfloat16)
    tail = lax.dot_general(tail_ref[...], weighted, back, preferred_element_type=jnp.float32)
    tail = tail.reshape(segments, tails, levels)
    count = segments // CHUNKS
    stores = []
    for i in range(CHUNKS):
        part = pl.ds(i * count * HEAD, count * HEAD)
        head = lax.dot_general(head_ref[part], weighted, back, preferred_element_type=jnp.float32)
        head = squeeze(head.reshape(count, HEAD, levels), tail[i * count : (i + 1) * count])
        result[part] = head.reshape(count * HEAD, levels).astype(jnp.bfloat16)
        stores.append(pltpu.make_async_copy(result.at[part], out_ref.at[part], out_sems.at[i]))
        stores[i].start()
    for store in stores:
        store.wait()


def finish_kernel(late, waiting_bands, fields, *refs):
    refs = list(refs)
    low_ref, factor_ref, tend_ref, wind_hbm, tracer_hbm, high_ref, side_ref, below_ref, top_ref = refs[:9]
    refs = refs[9:]
    lat = lax.axis_index("lat")
    lat_rows = tend_ref.shape[2]
    if late:
        next_low_ref, _, _, filt_hbm, out_hbm = refs[:5]
        refs = refs[5:]
        due = lat < waiting_bands
    else:
        filt_hbm, out_hbm, first_ref = refs[:3]
        refs = refs[3:]
        next_low_ref = None
        due = lat >= waiting_bands
        first_ref[0] = low_ref[lat_rows]
        first_ref[1] = low_ref[fields * lat_rows]

    @pl.when(due)
    def _():
        finish(
            lat,
            low_ref,
            factor_ref,
            tend_ref,
            wind_hbm,
            tracer_hbm,
            high_ref,
            side_ref,
            below_ref,
            top_ref,
            next_low_ref,
            filt_hbm,
            out_hbm,
            *refs,
        )


def finish(
    lat,
    low_ref,
    factor_ref,
    tend_ref,
    wind_hbm,
    tracer_hbm,
    high_ref,
    side_ref,
    below_ref,
    top_ref,
    next_low_ref,
    filt_hbm,
    out_hbm,
    wide_ref,
    rest_ref,
    filt,
    wind_ref,
    courant_ref,
    tracer_ref,
    out_ref,
    north_ref,
    below_wide,
    top_wide,
    filt_sems,
    wind_sems,
    in_sems,
    out_sems,
):
    fields, width, lat_rows, levels = tend_ref.shape
    count = tracer_ref.shape[0]
    size = width * lat_rows
    pieces = width // COLS
    winds = [pltpu.make_async_copy(wind_hbm.at[f], wind_ref.at[f], wind_sems.at[f]) for f in range(2)]
    loads = []
    stores = []
    for i in range(pieces):
        part = pl.ds(i * COLS, COLS)
        loads.append(
            pltpu.make_async_copy(tracer_hbm.at[:, part], tracer_ref.at[:, part], in_sems.at[i])
        )
        stores.append(pltpu.make_async_copy(out_ref.at[:, part], out_hbm.at[:, part], out_sems.at[i]))
    for load in winds + loads[::-1]:
        load.start()
    damp, face, face_next, inverse = (
        jnp.broadcast_to(factor_ref[lat, i], (lat_rows, levels)) for i in range(4)
    )

    for r in range(lat_rows):
        rest_ref[r] = expand(low_ref[fields * lat_rows + r].astype(jnp.float32))
    for f in range(fields):
        for r in range(lat_rows):
            row = expand(low_ref[f * lat_rows + r].astype(jnp.float32))
            wide_ref[f, pl.ds(r, SEG, stride=lat_rows), :] = with_rest(row, rest_ref[r], f)
        low = wide_ref[f, :size].reshape(width, lat_rows, levels)
        value = (damp[None] * tend_ref[f].astype(jnp.float32) + low).astype(jnp.bfloat16)
        filt[f] = value
        stores.append(pltpu.make_async_copy(filt.at[f], filt_hbm.at[f], filt_sems.at[f]))
        stores[-1].start()
        if f < 2:
            winds[f].wait()
            courant_ref[f, :width] = (0.5, 0.25)[f] * jnp.tanh(wind_ref[f] + value.astype(jnp.float32))
        if f == 0:
            edge = damp * high_ref[count + 1].astype(jnp.float32) + wide_ref[f, size : size + lat_rows]
            edge = edge.astype(jnp.bfloat16).astype(jnp.float32)
            courant_ref[f, width] = 0.5 * jnp.tanh(high_ref[count].astype(jnp.float32) + edge)

    sublane = lax.broadcasted_iota(jnp.int32, (lat_rows, levels), 0)
    is_first = sublane == 0
    is_last = sublane == lat_rows - 1
    below_wide[:, :width] = below_ref[...].astype(jnp.float32)
    top_wide[:, :width] = top_ref[...].astype(jnp.float32)
    edge = factor_ref[lat, 4, 0:1] * below_wide[count + 1, :width]
    if next_low_ref is not None:
        row, rest = (expand(next_low_ref[i].astype(jnp.float32)) for i in range(2))
        edge += with_rest(row, rest, 1)[:width]
    edge = edge.astype(jnp.bfloat16).astype(jnp.float32)
    north_ref[:width] = 0.25 * jnp.tanh(below_wide[count, :width] + edge)
    loads[pieces - 1].wait()
    east = courant_ref[0, width]
    flux = [
        jnp.maximum(east, 0.0) * tracer_ref[q, width - 1]
        + jnp.minimum(east, 0.0) * high_ref[q].astype(jnp.float32)
        for q in range(count)
    ]
    for piece in reversed(range(pieces)):
        if piece > 0:
            loads[piece - 1].wait()
        for column in reversed(range(piece * COLS, (piece + 1) * COLS)):
            east = courant_ref[0, column]
            north = courant_ref[1, column]
            north_next = jnp.where(
                is_last, north_ref[column : column + 1], pltpu.roll(north, lat_rows - 1, 0)
            )
            west_plus = jnp.maximum(east, 0.0)
            west_minus = jnp.minimum(east, 0.0)
            pole_plus = face * jnp.maximum(north, 0.0)
            pole_minus = face * jnp.minimum(north, 0.0)
            next_plus = face_next * jnp.maximum(north_next, 0.0)
            next_minus = face_next * jnp.minimum(north_next, 0.0)
            for q in range(count):
                here = tracer_ref[q, column]
                if column > 0:
                    west = tracer_ref[q, column - 1]
                else:
                    west = side_ref[q].astype(jnp.float32)
                prior = jnp.where(
                    is_first, top_wide[q, column : column + 1], pltpu.roll(here, 1, 0)
                )
                after = jnp.where(
                    is_last, below_wide[q, column : column + 1], pltpu.roll(here, lat_rows - 1, 0)
                )
                f_west = west_plus * west + west_minus * here
                g_pole = pole_plus * prior + pole_minus * here
                g_next = next_plus * here + next_minus * after
                out_ref[q, column] = here - (flux[q] - f_west) - (g_next - g_pole) * inverse
                flux[q] = f_west
        stores[piece].start()
    for store in stores:
        store.wait()


def row_factors(lat_devices, lat_rows):
    ids = np.arange(lat_devices * lat_rows + 1)
    half = lat_devices * lat_rows // 2
    damping = np.where(ids < half, 0.25 + 0.5 * (ids + 0.5) / half, 1.0)
    grid_row = ids + HEMI // 2 - half
    face = np.sin(math.pi * grid_row / (2.0 * HEMI))
    centre = np.sin(math.pi * (grid_row + 0.5) / (2.0 * HEMI))
    rows = np.stack(
        [damping[:-1], face[:-1], face[1:], 1.0 / centre[:-1], np.repeat(damping[lat_rows::lat_rows], lat_rows)]
    )
    rows = rows.reshape(5, lat_devices, lat_rows).swapaxes(0, 1).astype(np.float32)
    return rows[..., None]


def in_vmem(array):
    return pltpu.with_memory_space_constraint(array, pltpu.VMEM)


def in_hbm(array):
    return pltpu.with_memory_space_constraint(array, pltpu.HBM)


def per_device(tendencies, bands, winds, tracers):
    fields, lat_rows, width, levels = tendencies.shape
    count = tracers.shape[0]
    lat_devices = lax.axis_size("lat")
    segments = lax.axis_size("lon")
    lat_place = lax.axis_index("lat")
    lon_place = lax.axis_index("lon")
    tendencies, winds, tracers = (a.transpose(0, 2, 1, 3) for a in (tendencies, winds, tracers))

    to_prior = [(i + 1, i) for i in range(lat_devices - 1)]
    to_next = [(i, i + 1) for i in range(lat_devices - 1)]
    west_ring = [((i + 1) % segments, i) for i in range(segments)]
    east_ring = [(i, (i + 1) % segments) for i in range(segments)]
    vmem = pl.BlockSpec(memory_space=pltpu.VMEM)
    hbm = pl.BlockSpec(memory_space=pltpu.HBM)
    params = pltpu.CompilerParams(vmem_limit_bytes=LIMIT)
    bf16 = jnp.bfloat16

    send = pl.pallas_call(
        pack_kernel,
        in_specs=[hbm],
        out_specs=hbm,
        out_shape=pltpu.HBM((segments, HEAD, levels), bf16),
        scratch_shapes=[
            pltpu.VMEM(tendencies.shape, bf16),
            pltpu.VMEM((fields, SEG * lat_rows, levels), jnp.float32),
            pltpu.VMEM((segments, HEAD, levels), bf16),
            pltpu.SemaphoreType.DMA((fields,)),
            pltpu.SemaphoreType.DMA((segments // lat_rows,)),
        ],
        compiler_params=params,
        name="pack",
    )(in_hbm(tendencies))
    with jax.named_scope("forth"):
        rows = lax.all_to_all(send, "lon", split_axis=0, concat_axis=0, tiled=True)

    factors = jnp.asarray(row_factors(lat_devices, lat_rows))
    (p_one, p_two, q_one, q_two), waves, used = trig_tables(segments * width, segments)
    row = lat_place * lat_rows + lon_place % lat_rows
    half = lat_devices * lat_rows // 2
    damping = 0.25 + 0.5 * (row.astype(jnp.float32) + 0.5) / half
    damping = jnp.where(row < half, damping, 1.0)
    fold = np.where(used, np.where(waves == 0, 1.0, 2.0), 0.0) / (segments * width)
    weight = (1.0 - damping) * jnp.asarray(fold, jnp.float32)[None]
    weight = jnp.where(jnp.asarray(waves)[None] <= bands[row], weight, 0.0)
    with jax.named_scope("table"):
        head_table, tail_table = (
            (
                jnp.asarray(p_one)[:, None, :] * jnp.asarray(q_one[part])[None, :, :]
                + jnp.asarray(p_two)[:, None, :] * jnp.asarray(q_two[part])[None, :, :]
            )
            .astype(bf16)
            .reshape(-1, COEF)
            for part in (slice(0, HEAD), slice(HEAD, SEG))
        )

    with jax.named_scope("edges"):
        high = jnp.concatenate(
            [tracers[:, 0].astype(bf16), winds[0:1, 0].astype(bf16), tendencies[0:1, 0]], axis=0
        )
        side = tracers[:, width - 1].astype(bf16)
        below = jnp.concatenate(
            [tracers[:, :, 0].astype(bf16), winds[1:2, :, 0].astype(bf16), tendencies[1:2, :, 0]], axis=0
        )
        top = tracers[:, :, lat_rows - 1].astype(bf16)
    with jax.named_scope("columns"):
        high = lax.ppermute(high, "lon", west_ring)
        side = lax.ppermute(side, "lon", east_ring)
    rows, head_table, tail_table, weight, high, side, below, top = lax.optimization_barrier(
        (rows, head_table, tail_table, weight, high, side, below, top)
    )

    low = pl.pallas_call(
        transform_kernel,
        in_specs=[hbm, vmem, vmem, vmem],
        out_specs=hbm,
        out_shape=pltpu.HBM((segments * HEAD, levels), bf16),
        scratch_shapes=[
            pltpu.VMEM((segments * HEAD, levels), bf16),
            pltpu.VMEM((segments * HEAD, levels), bf16),
            pltpu.SemaphoreType.DMA((LOADS,)),
            pltpu.SemaphoreType.DMA((CHUNKS,)),
        ],
        compiler_params=params,
        name="transform",
    )(
        in_hbm(rows.reshape(segments * HEAD, levels)),
        in_vmem(weight),
        in_vmem(head_table),
        in_vmem(tail_table),
    )
    low, below, top = lax.optimization_barrier((low, below, top))
    with jax.named_scope("back"):
        low = lax.all_to_all(
            low.reshape(segments, HEAD, levels), "lon", split_axis=0, concat_axis=0, tiled=True
        )
    with jax.named_scope("below"):
        below = lax.ppermute(below, "lat", to_prior)
    with jax.named_scope("top"):
        top = lax.ppermute(top, "lat", to_next)
    waiting = lat_devices // 2 - 1
    outs = [pltpu.HBM(tendencies.shape, bf16), pltpu.HBM(tracers.shape, jnp.float32)]
    scratch = [
        pltpu.VMEM((fields, SEG * lat_rows, levels), jnp.float32),
        pltpu.VMEM((lat_rows, SEG, levels), jnp.float32),
        pltpu.VMEM(tendencies.shape, bf16),
        pltpu.VMEM(winds.shape, jnp.float32),
        pltpu.VMEM((2, width + 1, lat_rows, levels), jnp.float32),
        pltpu.VMEM(tracers.shape, jnp.float32),
        pltpu.VMEM(tracers.shape, jnp.float32),
        pltpu.VMEM((SEG, levels), jnp.float32),
        pltpu.VMEM((count + 2, SEG, levels), jnp.float32),
        pltpu.VMEM((count, SEG, levels), jnp.float32),
        pltpu.SemaphoreType.DMA((fields,)),
        pltpu.SemaphoreType.DMA((2,)),
        pltpu.SemaphoreType.DMA((width // COLS,)),
        pltpu.SemaphoreType.DMA((width // COLS,)),
    ]
    operands = (
        in_vmem(low),
        in_vmem(factors),
        in_vmem(tendencies),
        in_hbm(winds),
        in_hbm(tracers),
        in_vmem(high),
        in_vmem(side),
        in_vmem(below),
        in_vmem(top),
    )
    specs = [vmem] * 3 + [hbm] * 2 + [vmem] * 4
    filtered, advected, first = pl.pallas_call(
        functools.partial(finish_kernel, False, waiting, fields),
        in_specs=specs,
        out_specs=[hbm, hbm, vmem],
        out_shape=outs + [jax.ShapeDtypeStruct((2, HEAD, levels), bf16)],
        scratch_shapes=scratch,
        compiler_params=params,
        name="early",
    )(*operands)
    next_low = lax.ppermute(first, "lat", to_prior[:waiting])
    filtered, advected = pl.pallas_call(
        functools.partial(finish_kernel, True, waiting, fields),
        in_specs=specs + [vmem, hbm, hbm],
        out_specs=[hbm, hbm],
        out_shape=outs,
        scratch_shapes=scratch,
        input_output_aliases={10: 0, 11: 1},
        compiler_params=params,
        name="late",
    )(*operands, in_vmem(next_low), filtered, advected)
    return (filtered.transpose(0, 2, 1, 3), advected.transpose(0, 2, 1, 3))


def solution(mesh):
    return jax.shard_map(
        per_device,
        mesh=mesh,
        in_specs=(
            P(None, "lat", "lon", None),
            P(),
            P(None, "lat", "lon", None),
            P(None, "lat", "lon", None),
        ),
        out_specs=(P(None, "lat", "lon", None), P(None, "lat", "lon", None)),
        check_vma=False,
    )
```

```python
import functools
import math

import jax
import jax.numpy as jnp
import numpy as np
from jax import lax
from jax.experimental import pallas as pl
from jax.experimental.pallas import tpu as pltpu
from jax.sharding import PartitionSpec as P

HEMI = 720
KMAX = 180
COEF = 384
SEG = 48
HEAD = 40
QUARTER = 32
MAIN = 96
LIMIT = 24 << 20
LOADS = 5
CHUNKS = 4
COLS = 9


def trig_tables(lon_count, segments):
    width = lon_count // segments
    k = np.zeros(COEF)
    k[: KMAX + 1] = np.arange(KMAX + 1)
    k[KMAX + 1 : 2 * KMAX + 1] = np.arange(1, KMAX + 1)
    is_cos = np.zeros(COEF, bool)
    is_cos[: KMAX + 1] = True
    used = np.arange(COEF) < 2 * KMAX + 1
    over_p = 2 * np.pi * np.outer(np.arange(segments) * width, k) / lon_count
    over_q = 2 * np.pi * np.outer(np.arange(SEG), k) / lon_count
    p_one = np.where(is_cos, np.cos(over_p), np.sin(over_p)) * used
    p_two = np.where(is_cos, -np.sin(over_p), np.cos(over_p)) * used
    tables = (p_one, p_two, np.cos(over_q), np.sin(over_q))
    return tuple(t.astype(np.float32) for t in tables), k.astype(np.int32), used


def squeeze(head, tail):
    lane = lax.broadcasted_iota(jnp.int32, tail.shape, tail.ndim - 1)
    size = tail.shape[-2]
    groups = [
        jnp.where(
            lane < MAIN,
            head[..., i * size : (i + 1) * size, :],
            pltpu.roll(tail, MAIN - i * QUARTER, tail.ndim - 1),
        )
        for i in range(MAIN // QUARTER)
    ]
    return jnp.concatenate(groups + [head[..., MAIN // QUARTER * size :, :]], axis=-2)


def tail_of(head):
    size = SEG - HEAD
    moved = [
        pltpu.roll(head[..., i * size : (i + 1) * size, :], (i + 1) * QUARTER, head.ndim - 1)
        for i in range(MAIN // QUARTER)
    ]
    lane = lax.broadcasted_iota(jnp.int32, moved[0].shape, head.ndim - 1)
    return jnp.where(lane < QUARTER, moved[0], jnp.where(lane < 2 * QUARTER, moved[1], moved[2]))


def expand(head):
    return jnp.concatenate([head, tail_of(head)], axis=-2)


def with_rest(row, rest, f):
    lane = lax.broadcasted_iota(jnp.int32, row.shape, row.ndim - 1)
    return jnp.where(lane < MAIN, row, pltpu.roll(rest, MAIN - f * QUARTER, row.ndim - 1))


def pack_kernel(tend_ref, out_ref, tend, wide, rows, in_sems, out_sems):
    fields, width, lat_rows, levels = tend.shape
    size = width * lat_rows
    loads = [pltpu.make_async_copy(tend_ref.at[f], tend.at[f], in_sems.at[f]) for f in range(fields)]
    for load in loads:
        load.start()
    stores = []

    def send(block):
        part = pl.ds(block * lat_rows, lat_rows)
        store = pltpu.make_async_copy(rows.at[part], out_ref.at[part], out_sems.at[block])
        store.start()
        stores.append(store)

    for f in range(fields):
        wide[f, size:] = jnp.zeros((SEG * lat_rows - size, levels), jnp.float32)
    for f in range(fields):
        loads[f].wait()
        wide[f, :size] = tend[f].astype(jnp.float32).reshape(size, levels)
        for r in range(lat_rows):
            row = wide[f, pl.ds(r, SEG, stride=lat_rows), :]
            rows[f * lat_rows + r] = squeeze(row[:HEAD], row[HEAD:]).astype(jnp.bfloat16)
        send(f)
    lane = lax.broadcasted_iota(jnp.int32, (SEG, levels), 1)
    for r in range(lat_rows):
        moved = [
            pltpu.roll(wide[f, pl.ds(r, SEG, stride=lat_rows), :], (f + 1) * QUARTER, 1)
            for f in range(fields)
        ]
        row = jnp.where(lane < QUARTER, moved[0], jnp.where(lane < 2 * QUARTER, moved[1], moved[2]))
        rows[fields * lat_rows + r] = squeeze(row[:HEAD], row[HEAD:]).astype(jnp.bfloat16)
    send(fields)
    for store in stores:
        store.wait()


def transform_kernel(
    rows_ref, weight_ref, head_ref, tail_ref, out_ref, rows, result, in_sems, out_sems
):
    total, levels = rows.shape
    tails = SEG - HEAD
    segments = total // HEAD
    piece = total // LOADS
    loads = [
        pltpu.make_async_copy(
            rows_ref.at[pl.ds(i * piece, piece)], rows.at[pl.ds(i * piece, piece)], in_sems.at[i]
        )
        for i in range(LOADS)
    ]
    for load in loads:
        load.start()
    forward = (((0,), (0,)), ((), ()))
    back = (((1,), (1,)), ((), ()))
    spectrum = 0.0
    for i, load in enumerate(loads):
        load.wait()
        part = pl.ds(i * piece, piece)
        spectrum += lax.dot_general(
            rows[part], head_ref[part], forward, preferred_element_type=jnp.float32
        )
    tail = tail_of(rows[...].astype(jnp.float32).reshape(segments, HEAD, levels))
    tail = tail.reshape(segments * tails, levels).astype(jnp.bfloat16)
    spectrum += lax.dot_general(tail, tail_ref[...], forward, preferred_element_type=jnp.float32)
    weighted = (spectrum * weight_ref[...]).astype(jnp.bfloat16)
    tail = lax.dot_general(tail_ref[...], weighted, back, preferred_element_type=jnp.float32)
    tail = tail.reshape(segments, tails, levels)
    count = segments // CHUNKS
    stores = []
    for i in range(CHUNKS):
        part = pl.ds(i * count * HEAD, count * HEAD)
        head = lax.dot_general(head_ref[part], weighted, back, preferred_element_type=jnp.float32)
        head = squeeze(head.reshape(count, HEAD, levels), tail[i * count : (i + 1) * count])
        result[part] = head.reshape(count * HEAD, levels).astype(jnp.bfloat16)
        stores.append(pltpu.make_async_copy(result.at[part], out_ref.at[part], out_sems.at[i]))
        stores[i].start()
    for store in stores:
        store.wait()


def early_kernel(
    waiting,
    low_ref,
    factor_ref,
    tend_ref,
    wind_hbm,
    tracer_hbm,
    high_ref,
    side_ref,
    below_ref,
    top_ref,
    filt_hbm,
    out_hbm,
    first_ref,
    courant_ref,
    tracer_ref,
    *scratch,
):
    fields, _, lat_rows, _ = tend_ref.shape
    lat = lax.axis_index("lat")
    first_ref[0] = low_ref[lat_rows]
    first_ref[1] = low_ref[fields * lat_rows]
    add_scratch, advect_scratch = scratch[:6], scratch[6:]

    @pl.when(lat >= waiting)
    def _():
        loads = tracer_loads(tracer_hbm, tracer_ref, add_scratch[5])
        for load in loads[::-1]:
            load.start()
        stores = add_rows(
            lat, low_ref, factor_ref, tend_ref, wind_hbm, high_ref, filt_hbm, courant_ref, *add_scratch[:5]
        )
        advect(
            lat,
            factor_ref,
            courant_ref,
            tracer_ref,
            high_ref,
            side_ref,
            below_ref,
            top_ref,
            None,
            loads,
            out_hbm,
            *advect_scratch,
        )
        for store in stores:
            store.wait()


def middle_kernel(
    waiting,
    low_ref,
    factor_ref,
    tend_ref,
    wind_hbm,
    tracer_hbm,
    high_ref,
    _,
    filt_hbm,
    courant_ref,
    tracer_ref,
    *scratch,
):
    lat = lax.axis_index("lat")

    @pl.when(lat < waiting)
    def _():
        loads = tracer_loads(tracer_hbm, tracer_ref, scratch[5])
        for load in loads:
            load.start()
        stores = add_rows(
            lat, low_ref, factor_ref, tend_ref, wind_hbm, high_ref, filt_hbm, courant_ref, *scratch[:5]
        )
        for copy in loads + stores:
            copy.wait()


def late_kernel(
    waiting,
    factor_ref,
    courant_ref,
    tracer_ref,
    high_ref,
    side_ref,
    below_ref,
    top_ref,
    next_low_ref,
    _,
    out_hbm,
    *scratch,
):
    lat = lax.axis_index("lat")

    @pl.when(lat < waiting)
    def _():
        advect(
            lat,
            factor_ref,
            courant_ref,
            tracer_ref,
            high_ref,
            side_ref,
            below_ref,
            top_ref,
            next_low_ref,
            None,
            out_hbm,
            *scratch,
        )


def tracer_loads(tracer_hbm, tracer_ref, sems):
    return [
        pltpu.make_async_copy(
            tracer_hbm.at[:, pl.ds(i * COLS, COLS)], tracer_ref.at[:, pl.ds(i * COLS, COLS)], sems.at[i]
        )
        for i in range(tracer_ref.shape[1] // COLS)
    ]


def add_rows(
    lat,
    low_ref,
    factor_ref,
    tend_ref,
    wind_hbm,
    high_ref,
    filt_hbm,
    courant_ref,
    wide_ref,
    rest_ref,
    filt,
    wind_ref,
    sems,
):
    fields, width, lat_rows, levels = tend_ref.shape
    count = high_ref.shape[0] - 2
    size = width * lat_rows
    winds = [
        pltpu.make_async_copy(wind_hbm.at[f], wind_ref.at[f], sems.at[fields + f]) for f in range(2)
    ]
    for load in winds:
        load.start()
    stores = []
    damp = jnp.broadcast_to(factor_ref[lat, 0], (lat_rows, levels))

    for r in range(lat_rows):
        rest_ref[r] = expand(low_ref[fields * lat_rows + r].astype(jnp.float32))
    for f in range(fields):
        for r in range(lat_rows):
            row = expand(low_ref[f * lat_rows + r].astype(jnp.float32))
            wide_ref[f, pl.ds(r, SEG, stride=lat_rows), :] = with_rest(row, rest_ref[r], f)
        low = wide_ref[f, :size].reshape(width, lat_rows, levels)
        value = (damp[None] * tend_ref[f].astype(jnp.float32) + low).astype(jnp.bfloat16)
        filt[f] = value
        stores.append(pltpu.make_async_copy(filt.at[f], filt_hbm.at[f], sems.at[f]))
        stores[-1].start()
        if f < 2:
            winds[f].wait()
            courant_ref[f, :width] = (0.5, 0.25)[f] * jnp.tanh(wind_ref[f] + value.astype(jnp.float32))
        if f == 0:
            edge = damp * high_ref[count + 1].astype(jnp.float32) + wide_ref[f, size : size + lat_rows]
            edge = edge.astype(jnp.bfloat16).astype(jnp.float32)
            courant_ref[f, width] = 0.5 * jnp.tanh(high_ref[count].astype(jnp.float32) + edge)
    return stores


def advect(
    lat,
    factor_ref,
    courant_ref,
    tracer_ref,
    high_ref,
    side_ref,
    below_ref,
    top_ref,
    next_low_ref,
    loads,
    out_hbm,
    out_ref,
    north_ref,
    below_wide,
    top_wide,
    sems,
):
    count, width, lat_rows, levels = tracer_ref.shape
    pieces = width // COLS
    stores = [
        pltpu.make_async_copy(
            out_ref.at[:, pl.ds(i * COLS, COLS)], out_hbm.at[:, pl.ds(i * COLS, COLS)], sems.at[i]
        )
        for i in range(pieces)
    ]
    face, face_next, inverse = (
        jnp.broadcast_to(factor_ref[lat, i], (lat_rows, levels)) for i in (1, 2, 3)
    )
    sublane = lax.broadcasted_iota(jnp.int32, (lat_rows, levels), 0)
    is_first = sublane == 0
    is_last = sublane == lat_rows - 1
    below_wide[:, :width] = below_ref[...].astype(jnp.float32)
    top_wide[:, :width] = top_ref[...].astype(jnp.float32)
    edge = factor_ref[lat, 4, 0:1] * below_wide[count + 1, :width]
    if next_low_ref is not None:
        row, rest = (expand(next_low_ref[i].astype(jnp.float32)) for i in range(2))
        edge += with_rest(row, rest, 1)[:width]
    edge = edge.astype(jnp.bfloat16).astype(jnp.float32)
    north_ref[:width] = 0.25 * jnp.tanh(below_wide[count, :width] + edge)
    if loads is not None:
        loads[pieces - 1].wait()
    east = courant_ref[0, width]
    flux = [
        jnp.maximum(east, 0.0) * tracer_ref[q, width - 1]
        + jnp.minimum(east, 0.0) * high_ref[q].astype(jnp.float32)
        for q in range(count)
    ]
    for piece in reversed(range(pieces)):
        if piece > 0 and loads is not None:
            loads[piece - 1].wait()
        for column in reversed(range(piece * COLS, (piece + 1) * COLS)):
            east = courant_ref[0, column]
            north = courant_ref[1, column]
            north_next = jnp.where(
                is_last, north_ref[column : column + 1], pltpu.roll(north, lat_rows - 1, 0)
            )
            west_plus = jnp.maximum(east, 0.0)
            west_minus = jnp.minimum(east, 0.0)
            pole_plus = face * jnp.maximum(north, 0.0)
            pole_minus = face * jnp.minimum(north, 0.0)
            next_plus = face_next * jnp.maximum(north_next, 0.0)
            next_minus = face_next * jnp.minimum(north_next, 0.0)
            for q in range(count):
                here = tracer_ref[q, column]
                if column > 0:
                    west = tracer_ref[q, column - 1]
                else:
                    west = side_ref[q].astype(jnp.float32)
                prior = jnp.where(
                    is_first, top_wide[q, column : column + 1], pltpu.roll(here, 1, 0)
                )
                after = jnp.where(
                    is_last, below_wide[q, column : column + 1], pltpu.roll(here, lat_rows - 1, 0)
                )
                f_west = west_plus * west + west_minus * here
                g_pole = pole_plus * prior + pole_minus * here
                g_next = next_plus * here + next_minus * after
                out_ref[q, column] = here - (flux[q] - f_west) - (g_next - g_pole) * inverse
                flux[q] = f_west
        stores[piece].start()
    for store in stores:
        store.wait()


def row_factors(lat_devices, lat_rows):
    ids = np.arange(lat_devices * lat_rows + 1)
    half = lat_devices * lat_rows // 2
    damping = np.where(ids < half, 0.25 + 0.5 * (ids + 0.5) / half, 1.0)
    grid_row = ids + HEMI // 2 - half
    face = np.sin(math.pi * grid_row / (2.0 * HEMI))
    centre = np.sin(math.pi * (grid_row + 0.5) / (2.0 * HEMI))
    rows = np.stack(
        [damping[:-1], face[:-1], face[1:], 1.0 / centre[:-1], np.repeat(damping[lat_rows::lat_rows], lat_rows)]
    )
    rows = rows.reshape(5, lat_devices, lat_rows).swapaxes(0, 1).astype(np.float32)
    return rows[..., None]


def in_vmem(array):
    return pltpu.with_memory_space_constraint(array, pltpu.VMEM)


def in_hbm(array):
    return pltpu.with_memory_space_constraint(array, pltpu.HBM)


def per_device(tendencies, bands, winds, tracers):
    fields, lat_rows, width, levels = tendencies.shape
    count = tracers.shape[0]
    lat_devices = lax.axis_size("lat")
    segments = lax.axis_size("lon")
    lat_place = lax.axis_index("lat")
    lon_place = lax.axis_index("lon")
    tendencies, winds, tracers = (a.transpose(0, 2, 1, 3) for a in (tendencies, winds, tracers))

    to_prior = [(i + 1, i) for i in range(lat_devices - 1)]
    to_next = [(i, i + 1) for i in range(lat_devices - 1)]
    west_ring = [((i + 1) % segments, i) for i in range(segments)]
    east_ring = [(i, (i + 1) % segments) for i in range(segments)]
    vmem = pl.BlockSpec(memory_space=pltpu.VMEM)
    hbm = pl.BlockSpec(memory_space=pltpu.HBM)
    params = pltpu.CompilerParams(vmem_limit_bytes=LIMIT)
    bf16 = jnp.bfloat16

    send = pl.pallas_call(
        pack_kernel,
        in_specs=[hbm],
        out_specs=hbm,
        out_shape=pltpu.HBM((segments, HEAD, levels), bf16),
        scratch_shapes=[
            pltpu.VMEM(tendencies.shape, bf16),
            pltpu.VMEM((fields, SEG * lat_rows, levels), jnp.float32),
            pltpu.VMEM((segments, HEAD, levels), bf16),
            pltpu.SemaphoreType.DMA((fields,)),
            pltpu.SemaphoreType.DMA((segments // lat_rows,)),
        ],
        compiler_params=params,
        name="pack",
    )(in_hbm(tendencies))
    with jax.named_scope("forth"):
        rows = lax.all_to_all(send, "lon", split_axis=0, concat_axis=0, tiled=True)

    factors = jnp.asarray(row_factors(lat_devices, lat_rows))
    (p_one, p_two, q_one, q_two), waves, used = trig_tables(segments * width, segments)
    row = lat_place * lat_rows + lon_place % lat_rows
    half = lat_devices * lat_rows // 2
    damping = 0.25 + 0.5 * (row.astype(jnp.float32) + 0.5) / half
    damping = jnp.where(row < half, damping, 1.0)
    fold = np.where(used, np.where(waves == 0, 1.0, 2.0), 0.0) / (segments * width)
    weight = (1.0 - damping) * jnp.asarray(fold, jnp.float32)[None]
    weight = jnp.where(jnp.asarray(waves)[None] <= bands[row], weight, 0.0)
    with jax.named_scope("table"):
        head_table, tail_table = (
            (
                jnp.asarray(p_one)[:, None, :] * jnp.asarray(q_one[part])[None, :, :]
                + jnp.asarray(p_two)[:, None, :] * jnp.asarray(q_two[part])[None, :, :]
            )
            .astype(bf16)
            .reshape(-1, COEF)
            for part in (slice(0, HEAD), slice(HEAD, SEG))
        )

    with jax.named_scope("edges"):
        high = jnp.concatenate(
            [tracers[:, 0].astype(bf16), winds[0:1, 0].astype(bf16), tendencies[0:1, 0]], axis=0
        )
        side = tracers[:, width - 1].astype(bf16)
        below = jnp.concatenate(
            [tracers[:, :, 0].astype(bf16), winds[1:2, :, 0].astype(bf16), tendencies[1:2, :, 0]], axis=0
        )
        top = tracers[:, :, lat_rows - 1].astype(bf16)
    with jax.named_scope("columns"):
        high = lax.ppermute(high, "lon", west_ring)
        side = lax.ppermute(side, "lon", east_ring)
    rows, head_table, tail_table, weight, high, side, below, top = lax.optimization_barrier(
        (rows, head_table, tail_table, weight, high, side, below, top)
    )

    low = pl.pallas_call(
        transform_kernel,
        in_specs=[hbm, vmem, vmem, vmem],
        out_specs=hbm,
        out_shape=pltpu.HBM((segments * HEAD, levels), bf16),
        scratch_shapes=[
            pltpu.VMEM((segments * HEAD, levels), bf16),
            pltpu.VMEM((segments * HEAD, levels), bf16),
            pltpu.SemaphoreType.DMA((LOADS,)),
            pltpu.SemaphoreType.DMA((CHUNKS,)),
        ],
        compiler_params=params,
        name="transform",
    )(
        in_hbm(rows.reshape(segments * HEAD, levels)),
        in_vmem(weight),
        in_vmem(head_table),
        in_vmem(tail_table),
    )
    low, below, top = lax.optimization_barrier((low, below, top))
    with jax.named_scope("back"):
        low = lax.all_to_all(
            low.reshape(segments, HEAD, levels), "lon", split_axis=0, concat_axis=0, tiled=True
        )
    with jax.named_scope("below"):
        below = lax.ppermute(below, "lat", to_prior)
    with jax.named_scope("top"):
        top = lax.ppermute(top, "lat", to_next)
    waiting = lat_devices // 2 - 1
    filtered_out = pltpu.HBM(tendencies.shape, bf16)
    advected_out = pltpu.HBM(tracers.shape, jnp.float32)
    on_chip = [
        pltpu.VMEM((2, width + 1, lat_rows, levels), jnp.float32),
        pltpu.VMEM(tracers.shape, jnp.float32),
    ]
    add_scratch = [
        pltpu.VMEM((fields, SEG * lat_rows, levels), jnp.float32),
        pltpu.VMEM((lat_rows, SEG, levels), jnp.float32),
        pltpu.VMEM(tendencies.shape, bf16),
        pltpu.VMEM(winds.shape, jnp.float32),
        pltpu.SemaphoreType.DMA((fields + 2,)),
        pltpu.SemaphoreType.DMA((width // COLS,)),
    ]
    advect_scratch = [
        pltpu.VMEM(tracers.shape, jnp.float32),
        pltpu.VMEM((SEG, levels), jnp.float32),
        pltpu.VMEM((count + 2, SEG, levels), jnp.float32),
        pltpu.VMEM((count, SEG, levels), jnp.float32),
        pltpu.SemaphoreType.DMA((width // COLS,)),
    ]
    factors, high, side, below, top = (in_vmem(a) for a in (factors, high, side, below, top))
    operands = (in_vmem(low), factors, in_vmem(tendencies), in_hbm(winds), in_hbm(tracers), high)
    specs = [vmem] * 3 + [hbm] * 2 + [vmem]
    filtered, advected, first = pl.pallas_call(
        functools.partial(early_kernel, waiting),
        in_specs=specs + [vmem] * 3,
        out_specs=[hbm, hbm, vmem],
        out_shape=[filtered_out, advected_out, jax.ShapeDtypeStruct((2, HEAD, levels), bf16)],
        scratch_shapes=on_chip + add_scratch + advect_scratch,
        compiler_params=params,
        name="early",
    )(*operands, side, below, top)
    next_low = lax.ppermute(first, "lat", to_prior[:waiting])
    filtered, courant, held = pl.pallas_call(
        functools.partial(middle_kernel, waiting),
        in_specs=specs + [hbm],
        out_specs=[hbm, vmem, vmem],
        out_shape=[filtered_out] + on_chip,
        scratch_shapes=add_scratch,
        input_output_aliases={6: 0},
        compiler_params=params,
        name="middle",
    )(*operands, filtered)
    advected = pl.pallas_call(
        functools.partial(late_kernel, waiting),
        in_specs=[vmem] * 8 + [hbm],
        out_specs=hbm,
        out_shape=advected_out,
        scratch_shapes=advect_scratch,
        input_output_aliases={8: 0},
        compiler_params=params,
        name="late",
    )(factors, courant, held, high, side, below, top, in_vmem(next_low), advected)
    return (filtered.transpose(0, 2, 1, 3), advected.transpose(0, 2, 1, 3))


def solution(mesh):
    return jax.shard_map(
        per_device,
        mesh=mesh,
        in_specs=(
            P(None, "lat", "lon", None),
            P(),
            P(None, "lat", "lon", None),
            P(None, "lat", "lon", None),
        ),
        out_specs=(P(None, "lat", "lon", None), P(None, "lat", "lon", None)),
        check_vma=False,
    )
```

```python
import functools
import math

import jax
import jax.numpy as jnp
import numpy as np
from jax import lax
from jax.experimental import pallas as pl
from jax.experimental.pallas import tpu as pltpu
from jax.sharding import PartitionSpec as P

HEMI = 720
KMAX = 180
COEF = 384
SEG = 48
HEAD = 36
PAIR = 2 * HEAD
QUARTER = 32
MAIN = 96
LIMIT = 24 << 20
LOADS = 3
CHUNKS = 4
COLS = 9


HEAD_ORDER = [(side, q) for side in range(2) for q in range(HEAD)]
TAIL_ORDER = [(side, q) for side in range(2) for q in range(HEAD, SEG)]


def wave_rows():
    k = np.zeros(COEF, np.int32)
    k[: KMAX + 1] = np.arange(KMAX + 1)
    k[KMAX + 1 : 2 * KMAX + 1] = np.arange(1, KMAX + 1)
    place = np.arange(COEF)
    return k, place <= KMAX, place < 2 * KMAX + 1


def trig_table(lon_count, segments, order):
    width = lon_count // segments
    k, is_cos, used = wave_rows()
    over_p = 2 * np.pi * np.outer(np.arange(0, segments, 2) * width, k) / lon_count
    over_q = 2 * np.pi * np.outer([side * width + q for side, q in order], k) / lon_count
    p_one = np.where(is_cos, np.cos(over_p), np.sin(over_p)) * used
    p_two = np.where(is_cos, -np.sin(over_p), np.cos(over_p)) * used
    p_one, p_two, q_one, q_two = (
        jnp.asarray(t, jnp.float32) for t in (p_one, p_two, np.cos(over_q), np.sin(over_q))
    )
    table = p_one[:, None, :] * q_one[None, :, :] + p_two[:, None, :] * q_two[None, :, :]
    return table.astype(jnp.bfloat16).reshape(-1, COEF)


def lanes(like):
    return lax.broadcasted_iota(jnp.int32, like.shape, like.ndim - 1)


def squeeze(head, tail):
    last = [pltpu.roll(tail, MAIN - i * QUARTER, tail.ndim - 1) for i in range(MAIN // QUARTER)]
    return jnp.where(lanes(head) < MAIN, head, jnp.concatenate(last, axis=-2))


def tail_of(head):
    size = SEG - HEAD
    moved = [
        pltpu.roll(head[..., i * size : (i + 1) * size, :], (i + 1) * QUARTER, head.ndim - 1)
        for i in range(MAIN // QUARTER)
    ]
    lane = lanes(moved[0])
    return jnp.where(lane < QUARTER, moved[0], jnp.where(lane < 2 * QUARTER, moved[1], moved[2]))


def halves(pair):
    size = pair.shape[-2] // 2
    return pair[..., :size, :], pair[..., size:, :]


def expand(pair):
    return [jnp.concatenate([head, tail_of(head)], axis=-2) for head in halves(pair)]


def with_rest(row, rest, f):
    return jnp.where(lanes(row) < MAIN, row, pltpu.roll(rest, MAIN - f * QUARTER, row.ndim - 1))


def pack_kernel(tend_ref, out_ref, tend, wide, rows, in_sems, out_sems):
    fields, width, lat_rows, levels = tend.shape
    size = width * lat_rows
    half = lat_rows // 2
    loads = [pltpu.make_async_copy(tend_ref.at[f], tend.at[f], in_sems.at[f]) for f in range(fields)]
    for load in loads:
        load.start()
    stores = []

    def send(block):
        part = pl.ds(block * half, half)
        store = pltpu.make_async_copy(rows.at[part], out_ref.at[part], out_sems.at[block])
        store.start()
        stores.append(store)

    def put(pair, *slots):
        slots = [squeeze(slot[:HEAD], slot[HEAD:]) for slot in slots]
        rows[pair] = jnp.concatenate(slots, axis=0).astype(jnp.bfloat16)

    def whole(f, r):
        return wide[f, pl.ds(r, SEG, stride=lat_rows), :]

    def left(r):
        moved = [pltpu.roll(whole(f, r), (f + 1) * QUARTER, 1) for f in range(fields)]
        lane = lanes(moved[0])
        return jnp.where(lane < QUARTER, moved[0], jnp.where(lane < 2 * QUARTER, moved[1], moved[2]))

    for f in range(fields):
        wide[f, size:] = jnp.zeros((SEG * lat_rows - size, levels), jnp.float32)
    for f in range(fields):
        loads[f].wait()
        wide[f, :size] = tend[f].astype(jnp.float32).reshape(size, levels)
        for r in range(half):
            put(f * half + r, whole(f, 2 * r), whole(f, 2 * r + 1))
        send(f)
    for r in range(half):
        put(fields * half + r, left(2 * r), left(2 * r + 1))
    send(fields)
    for store in stores:
        store.wait()


def transform_kernel(
    rows_ref, weight_ref, head_ref, tail_ref, out_ref, rows, result, in_sems, out_sems
):
    total, levels = rows.shape
    pairs = total // PAIR
    piece = total // LOADS
    loads = [
        pltpu.make_async_copy(
            rows_ref.at[pl.ds(i * piece, piece)], rows.at[pl.ds(i * piece, piece)], in_sems.at[i]
        )
        for i in range(LOADS)
    ]
    for load in loads:
        load.start()
    forward = (((0,), (0,)), ((), ()))
    back = (((1,), (1,)), ((), ()))
    spectrum = 0.0
    for i, load in enumerate(loads):
        load.wait()
        part = pl.ds(i * piece, piece)
        spectrum += lax.dot_general(
            rows[part], head_ref[part], forward, preferred_element_type=jnp.float32
        )
    tail = [tail_of(head) for head in halves(rows[...].astype(jnp.float32).reshape(pairs, PAIR, levels))]
    tail = jnp.concatenate(tail, axis=-2)
    tail = tail.reshape(tail_ref.shape[0], levels).astype(jnp.bfloat16)
    spectrum += lax.dot_general(tail, tail_ref[...], forward, preferred_element_type=jnp.float32)
    weighted = (spectrum * weight_ref[...]).astype(jnp.bfloat16)
    tail = lax.dot_general(tail_ref[...], weighted, back, preferred_element_type=jnp.float32)
    tail = tail.reshape(pairs, 2 * (SEG - HEAD), levels)
    count = pairs // CHUNKS
    stores = []
    for i in range(CHUNKS):
        part = pl.ds(i * count * PAIR, count * PAIR)
        head = lax.dot_general(head_ref[part], weighted, back, preferred_element_type=jnp.float32)
        head = halves(head.reshape(count, PAIR, levels))
        last = halves(tail[i * count : (i + 1) * count])
        head = jnp.concatenate([squeeze(h, t) for h, t in zip(head, last)], axis=-2)
        result[part] = head.reshape(count * PAIR, levels).astype(jnp.bfloat16)
        stores.append(pltpu.make_async_copy(result.at[part], out_ref.at[part], out_sems.at[i]))
        stores[i].start()
    for store in stores:
        store.wait()


def early_kernel(
    waiting,
    low_ref,
    factor_ref,
    tend_ref,
    wind_hbm,
    tracer_hbm,
    high_ref,
    side_ref,
    below_ref,
    top_ref,
    filt_hbm,
    out_hbm,
    first_ref,
    courant_ref,
    tracer_ref,
    *scratch,
):
    fields, _, lat_rows, _ = tend_ref.shape
    lat = lax.axis_index("lat")
    first_ref[0] = low_ref[lat_rows // 2]
    first_ref[1] = low_ref[fields * lat_rows // 2]
    add_scratch, advect_scratch = scratch[:6], scratch[6:]

    @pl.when(lat >= waiting)
    def _():
        loads = tracer_loads(tracer_hbm, tracer_ref, add_scratch[5])
        for load in loads[::-1]:
            load.start()
        stores = add_rows(
            lat, low_ref, factor_ref, tend_ref, wind_hbm, high_ref, filt_hbm, courant_ref, *add_scratch[:5]
        )
        advect(
            lat,
            factor_ref,
            courant_ref,
            tracer_ref,
            high_ref,
            side_ref,
            below_ref,
            top_ref,
            None,
            loads,
            out_hbm,
            *advect_scratch,
        )
        for store in stores:
            store.wait()


def middle_kernel(
    waiting,
    low_ref,
    factor_ref,
    tend_ref,
    wind_hbm,
    tracer_hbm,
    high_ref,
    _,
    filt_hbm,
    courant_ref,
    tracer_ref,
    *scratch,
):
    lat = lax.axis_index("lat")

    @pl.when(lat < waiting)
    def _():
        loads = tracer_loads(tracer_hbm, tracer_ref, scratch[5])
        for load in loads:
            load.start()
        stores = add_rows(
            lat, low_ref, factor_ref, tend_ref, wind_hbm, high_ref, filt_hbm, courant_ref, *scratch[:5]
        )
        for copy in loads + stores:
            copy.wait()


def late_kernel(
    waiting,
    factor_ref,
    courant_ref,
    tracer_ref,
    high_ref,
    side_ref,
    below_ref,
    top_ref,
    next_low_ref,
    _,
    out_hbm,
    *scratch,
):
    lat = lax.axis_index("lat")

    @pl.when(lat < waiting)
    def _():
        advect(
            lat,
            factor_ref,
            courant_ref,
            tracer_ref,
            high_ref,
            side_ref,
            below_ref,
            top_ref,
            next_low_ref,
            None,
            out_hbm,
            *scratch,
        )


def tracer_loads(tracer_hbm, tracer_ref, sems):
    return [
        pltpu.make_async_copy(
            tracer_hbm.at[:, pl.ds(i * COLS, COLS)], tracer_ref.at[:, pl.ds(i * COLS, COLS)], sems.at[i]
        )
        for i in range(tracer_ref.shape[1] // COLS)
    ]


def add_rows(
    lat,
    low_ref,
    factor_ref,
    tend_ref,
    wind_hbm,
    high_ref,
    filt_hbm,
    courant_ref,
    wide_ref,
    rest_ref,
    filt,
    wind_ref,
    sems,
):
    fields, width, lat_rows, levels = tend_ref.shape
    count = high_ref.shape[0] - 2
    size = width * lat_rows
    winds = [
        pltpu.make_async_copy(wind_hbm.at[f], wind_ref.at[f], sems.at[fields + f]) for f in range(2)
    ]
    for load in winds:
        load.start()
    stores = []
    damp = jnp.broadcast_to(factor_ref[lat, 0], (lat_rows, levels))

    half = lat_rows // 2
    for r in range(half):
        pair = expand(low_ref[fields * half + r].astype(jnp.float32))
        for i in range(2):
            rest_ref[2 * r + i] = pair[i]
    for f in range(fields):
        for r in range(half):
            pair = expand(low_ref[f * half + r].astype(jnp.float32))
            for i in range(2):
                row = with_rest(pair[i], rest_ref[2 * r + i], f)
                wide_ref[f, pl.ds(2 * r + i, SEG, stride=lat_rows), :] = row
        low = wide_ref[f, :size].reshape(width, lat_rows, levels)
        value = (damp[None] * tend_ref[f].astype(jnp.float32) + low).astype(jnp.bfloat16)
        filt[f] = value
        stores.append(pltpu.make_async_copy(filt.at[f], filt_hbm.at[f], sems.at[f]))
        stores[-1].start()
        if f < 2:
            winds[f].wait()
            courant_ref[f, :width] = (0.5, 0.25)[f] * jnp.tanh(wind_ref[f] + value.astype(jnp.float32))
        if f == 0:
            edge = damp * high_ref[count + 1].astype(jnp.float32) + wide_ref[f, size : size + lat_rows]
            edge = edge.astype(jnp.bfloat16).astype(jnp.float32)
            courant_ref[f, width] = 0.5 * jnp.tanh(high_ref[count].astype(jnp.float32) + edge)
    return stores


def advect(
    lat,
    factor_ref,
    courant_ref,
    tracer_ref,
    high_ref,
    side_ref,
    below_ref,
    top_ref,
    next_low_ref,
    loads,
    out_hbm,
    out_ref,
    north_ref,
    below_wide,
    top_wide,
    sems,
):
    count, width, lat_rows, levels = tracer_ref.shape
    pieces = width // COLS
    stores = [
        pltpu.make_async_copy(
            out_ref.at[:, pl.ds(i * COLS, COLS)], out_hbm.at[:, pl.ds(i * COLS, COLS)], sems.at[i]
        )
        for i in range(pieces)
    ]
    face, face_next, inverse = (
        jnp.broadcast_to(factor_ref[lat, i], (lat_rows, levels)) for i in (1, 2, 3)
    )
    sublane = lax.broadcasted_iota(jnp.int32, (lat_rows, levels), 0)
    is_first = sublane == 0
    is_last = sublane == lat_rows - 1
    below_wide[:, :width] = below_ref[...].astype(jnp.float32)
    top_wide[:, :width] = top_ref[...].astype(jnp.float32)
    edge = factor_ref[lat, 4, 0:1] * below_wide[count + 1, :width]
    if next_low_ref is not None:
        row, rest = (expand(next_low_ref[i].astype(jnp.float32))[0] for i in range(2))
        edge += with_rest(row, rest, 1)[:width]
    edge = edge.astype(jnp.bfloat16).astype(jnp.float32)
    north_ref[:width] = 0.25 * jnp.tanh(below_wide[count, :width] + edge)
    if loads is not None:
        loads[pieces - 1].wait()
    east = courant_ref[0, width]
    flux = [
        jnp.maximum(east, 0.0) * tracer_ref[q, width - 1]
        + jnp.minimum(east, 0.0) * high_ref[q].astype(jnp.float32)
        for q in range(count)
    ]
    for piece in reversed(range(pieces)):
        if piece > 0 and loads is not None:
            loads[piece - 1].wait()
        for column in reversed(range(piece * COLS, (piece + 1) * COLS)):
            east = courant_ref[0, column]
            north = courant_ref[1, column]
            north_next = jnp.where(
                is_last, north_ref[column : column + 1], pltpu.roll(north, lat_rows - 1, 0)
            )
            west_plus = jnp.maximum(east, 0.0)
            west_minus = jnp.minimum(east, 0.0)
            pole_plus = face * jnp.maximum(north, 0.0)
            pole_minus = face * jnp.minimum(north, 0.0)
            next_plus = face_next * jnp.maximum(north_next, 0.0)
            next_minus = face_next * jnp.minimum(north_next, 0.0)
            for q in range(count):
                here = tracer_ref[q, column]
                if column > 0:
                    west = tracer_ref[q, column - 1]
                else:
                    west = side_ref[q].astype(jnp.float32)
                prior = jnp.where(
                    is_first, top_wide[q, column : column + 1], pltpu.roll(here, 1, 0)
                )
                after = jnp.where(
                    is_last, below_wide[q, column : column + 1], pltpu.roll(here, lat_rows - 1, 0)
                )
                f_west = west_plus * west + west_minus * here
                g_pole = pole_plus * prior + pole_minus * here
                g_next = next_plus * here + next_minus * after
                out_ref[q, column] = here - (flux[q] - f_west) - (g_next - g_pole) * inverse
                flux[q] = f_west
        stores[piece].start()
    for store in stores:
        store.wait()


def row_factors(lat_devices, lat_rows):
    ids = np.arange(lat_devices * lat_rows + 1)
    half = lat_devices * lat_rows // 2
    damping = np.where(ids < half, 0.25 + 0.5 * (ids + 0.5) / half, 1.0)
    grid_row = ids + HEMI // 2 - half
    face = np.sin(math.pi * grid_row / (2.0 * HEMI))
    centre = np.sin(math.pi * (grid_row + 0.5) / (2.0 * HEMI))
    rows = np.stack(
        [damping[:-1], face[:-1], face[1:], 1.0 / centre[:-1], np.repeat(damping[lat_rows::lat_rows], lat_rows)]
    )
    rows = rows.reshape(5, lat_devices, lat_rows).swapaxes(0, 1).astype(np.float32)
    return rows[..., None]


def in_vmem(array):
    return pltpu.with_memory_space_constraint(array, pltpu.VMEM)


def in_hbm(array):
    return pltpu.with_memory_space_constraint(array, pltpu.HBM)


def per_device(tendencies, bands, winds, tracers):
    fields, lat_rows, width, levels = tendencies.shape
    count = tracers.shape[0]
    lat_devices = lax.axis_size("lat")
    segments = lax.axis_size("lon")
    lat_place = lax.axis_index("lat")
    lon_place = lax.axis_index("lon")
    tendencies, winds, tracers = (a.transpose(0, 2, 1, 3) for a in (tendencies, winds, tracers))

    to_prior = [(i + 1, i) for i in range(lat_devices - 1)]
    to_next = [(i, i + 1) for i in range(lat_devices - 1)]
    west_ring = [((i + 1) % segments, i) for i in range(segments)]
    east_ring = [(i, (i + 1) % segments) for i in range(segments)]
    vmem = pl.BlockSpec(memory_space=pltpu.VMEM)
    hbm = pl.BlockSpec(memory_space=pltpu.HBM)
    params = pltpu.CompilerParams(vmem_limit_bytes=LIMIT)
    bf16 = jnp.bfloat16
    total = segments // 2 * PAIR
    sent = (segments, HEAD // 4, 4, levels)

    send = pl.pallas_call(
        pack_kernel,
        in_specs=[hbm],
        out_specs=hbm,
        out_shape=pltpu.HBM((segments // 2, PAIR, levels), bf16),
        scratch_shapes=[
            pltpu.VMEM(tendencies.shape, bf16),
            pltpu.VMEM((fields, SEG * lat_rows, levels), jnp.float32),
            pltpu.VMEM((segments // 2, PAIR, levels), bf16),
            pltpu.SemaphoreType.DMA((fields,)),
            pltpu.SemaphoreType.DMA((segments // lat_rows,)),
        ],
        compiler_params=params,
        name="pack",
    )(in_hbm(tendencies))
    with jax.named_scope("forth"):
        rows = lax.all_to_all(send.reshape(sent), "lon", split_axis=0, concat_axis=0, tiled=True)

    factors = jnp.asarray(row_factors(lat_devices, lat_rows))
    waves, _, used = wave_rows()
    row = lat_place * lat_rows + lon_place % lat_rows
    half = lat_devices * lat_rows // 2
    damping = 0.25 + 0.5 * (row.astype(jnp.float32) + 0.5) / half
    damping = jnp.where(row < half, damping, 1.0)
    fold = np.where(used, np.where(waves == 0, 1.0, 2.0), 0.0) / (segments * width)
    weight = (1.0 - damping) * jnp.asarray(fold, jnp.float32)[None]
    weight = jnp.where(jnp.asarray(waves)[None] <= bands[row], weight, 0.0)
    with jax.named_scope("table"):
        head_table, tail_table = (
            trig_table(segments * width, segments, order) for order in (HEAD_ORDER, TAIL_ORDER)
        )

    with jax.named_scope("edges"):
        high = jnp.concatenate(
            [tracers[:, 0].astype(bf16), winds[0:1, 0].astype(bf16), tendencies[0:1, 0]], axis=0
        )
        side = tracers[:, width - 1].astype(bf16)
        below = jnp.concatenate(
            [tracers[:, :, 0].astype(bf16), winds[1:2, :, 0].astype(bf16), tendencies[1:2, :, 0]], axis=0
        )
        top = tracers[:, :, lat_rows - 1].astype(bf16)
    with jax.named_scope("columns"):
        high = lax.ppermute(high, "lon", west_ring)
        side = lax.ppermute(side, "lon", east_ring)
    rows, head_table, tail_table, weight, high, side, below, top = lax.optimization_barrier(
        (rows, head_table, tail_table, weight, high, side, below, top)
    )

    low = pl.pallas_call(
        transform_kernel,
        in_specs=[hbm, vmem, vmem, vmem],
        out_specs=hbm,
        out_shape=pltpu.HBM((total, levels), bf16),
        scratch_shapes=[
            pltpu.VMEM((total, levels), bf16),
            pltpu.VMEM((total, levels), bf16),
            pltpu.SemaphoreType.DMA((LOADS,)),
            pltpu.SemaphoreType.DMA((CHUNKS,)),
        ],
        compiler_params=params,
        name="transform",
    )(
        in_hbm(rows.reshape(total, levels)),
        in_vmem(weight),
        in_vmem(head_table),
        in_vmem(tail_table),
    )
    low, below, top = lax.optimization_barrier((low, below, top))
    with jax.named_scope("back"):
        low = lax.all_to_all(
            low.reshape(sent), "lon", split_axis=0, concat_axis=0, tiled=True
        ).reshape(segments // 2, PAIR, levels)
    with jax.named_scope("below"):
        below = lax.ppermute(below, "lat", to_prior)
    with jax.named_scope("top"):
        top = lax.ppermute(top, "lat", to_next)
    waiting = lat_devices // 2 - 1
    filtered_out = pltpu.HBM(tendencies.shape, bf16)
    advected_out = pltpu.HBM(tracers.shape, jnp.float32)
    on_chip = [
        pltpu.VMEM((2, width + 1, lat_rows, levels), jnp.float32),
        pltpu.VMEM(tracers.shape, jnp.float32),
    ]
    add_scratch = [
        pltpu.VMEM((fields, SEG * lat_rows, levels), jnp.float32),
        pltpu.VMEM((lat_rows, SEG, levels), jnp.float32),
        pltpu.VMEM(tendencies.shape, bf16),
        pltpu.VMEM(winds.shape, jnp.float32),
        pltpu.SemaphoreType.DMA((fields + 2,)),
        pltpu.SemaphoreType.DMA((width // COLS,)),
    ]
    advect_scratch = [
        pltpu.VMEM(tracers.shape, jnp.float32),
        pltpu.VMEM((SEG, levels), jnp.float32),
        pltpu.VMEM((count + 2, SEG, levels), jnp.float32),
        pltpu.VMEM((count, SEG, levels), jnp.float32),
        pltpu.SemaphoreType.DMA((width // COLS,)),
    ]
    factors, high, side, below, top = (in_vmem(a) for a in (factors, high, side, below, top))
    operands = (in_vmem(low), factors, in_vmem(tendencies), in_hbm(winds), in_hbm(tracers), high)
    specs = [vmem] * 3 + [hbm] * 2 + [vmem]
    filtered, advected, first = pl.pallas_call(
        functools.partial(early_kernel, waiting),
        in_specs=specs + [vmem] * 3,
        out_specs=[hbm, hbm, vmem],
        out_shape=[filtered_out, advected_out, jax.ShapeDtypeStruct((2, PAIR, levels), bf16)],
        scratch_shapes=on_chip + add_scratch + advect_scratch,
        compiler_params=params,
        name="early",
    )(*operands, side, below, top)
    next_low = lax.ppermute(first, "lat", to_prior[:waiting])
    filtered, courant, held = pl.pallas_call(
        functools.partial(middle_kernel, waiting),
        in_specs=specs + [hbm],
        out_specs=[hbm, vmem, vmem],
        out_shape=[filtered_out] + on_chip,
        scratch_shapes=add_scratch,
        input_output_aliases={6: 0},
        compiler_params=params,
        name="middle",
    )(*operands, filtered)
    advected = pl.pallas_call(
        functools.partial(late_kernel, waiting),
        in_specs=[vmem] * 8 + [hbm],
        out_specs=hbm,
        out_shape=advected_out,
        scratch_shapes=advect_scratch,
        input_output_aliases={8: 0},
        compiler_params=params,
        name="late",
    )(factors, courant, held, high, side, below, top, in_vmem(next_low), advected)
    return (filtered.transpose(0, 2, 1, 3), advected.transpose(0, 2, 1, 3))


def solution(mesh):
    return jax.shard_map(
        per_device,
        mesh=mesh,
        in_specs=(
            P(None, "lat", "lon", None),
            P(),
            P(None, "lat", "lon", None),
            P(None, "lat", "lon", None),
        ),
        out_specs=(P(None, "lat", "lon", None), P(None, "lat", "lon", None)),
        check_vma=False,
    )
```

```python
import functools
import math

import jax
import jax.numpy as jnp
import numpy as np
from jax import lax
from jax.experimental import pallas as pl
from jax.experimental.pallas import tpu as pltpu
from jax.sharding import PartitionSpec as P

HEMI = 720
KMAX = 180
COEF = 384
SEG = 48
HEAD = 36
PAIR = 2 * HEAD
QUARTER = 32
MAIN = 96
LIMIT = 24 << 20
LOADS = 3
CHUNKS = 4
COLS = 9


HEAD_ORDER = [(side, q) for side in range(2) for q in range(HEAD)]
TAIL_ORDER = [(side, q) for side in range(2) for q in range(HEAD, SEG)]


def wave_rows():
    k = np.zeros(COEF, np.int32)
    k[: KMAX + 1] = np.arange(KMAX + 1)
    k[KMAX + 1 : 2 * KMAX + 1] = np.arange(1, KMAX + 1)
    place = np.arange(COEF)
    return k, place <= KMAX, place < 2 * KMAX + 1


def trig_table(lon_count, segments, order):
    width = lon_count // segments
    k, is_cos, used = wave_rows()
    over_p = 2 * np.pi * np.outer(np.arange(0, segments, 2) * width, k) / lon_count
    over_q = 2 * np.pi * np.outer([side * width + q for side, q in order], k) / lon_count
    p_one = np.where(is_cos, np.cos(over_p), np.sin(over_p)) * used
    p_two = np.where(is_cos, -np.sin(over_p), np.cos(over_p)) * used
    p_one, p_two, q_one, q_two = (
        jnp.asarray(t, jnp.float32) for t in (p_one, p_two, np.cos(over_q), np.sin(over_q))
    )
    table = p_one[:, None, :] * q_one[None, :, :] + p_two[:, None, :] * q_two[None, :, :]
    return table.astype(jnp.bfloat16).reshape(-1, COEF)


def lanes(like):
    return lax.broadcasted_iota(jnp.int32, like.shape, like.ndim - 1)


def squeeze(head, tail):
    last = [pltpu.roll(tail, MAIN - i * QUARTER, tail.ndim - 1) for i in range(MAIN // QUARTER)]
    return jnp.where(lanes(head) < MAIN, head, jnp.concatenate(last, axis=-2))


def tail_of(head):
    size = SEG - HEAD
    moved = [
        pltpu.roll(head[..., i * size : (i + 1) * size, :], (i + 1) * QUARTER, head.ndim - 1)
        for i in range(MAIN // QUARTER)
    ]
    lane = lanes(moved[0])
    return jnp.where(lane < QUARTER, moved[0], jnp.where(lane < 2 * QUARTER, moved[1], moved[2]))


def halves(pair):
    size = pair.shape[-2] // 2
    return pair[..., :size, :], pair[..., size:, :]


def expand(pair):
    return [jnp.concatenate([head, tail_of(head)], axis=-2) for head in halves(pair)]


def with_rest(row, rest, f):
    return jnp.where(lanes(row) < MAIN, row, pltpu.roll(rest, MAIN - f * QUARTER, row.ndim - 1))


def pack_kernel(tend_ref, out_ref, tend, wide, rows, in_sems, out_sems):
    fields, width, lat_rows, levels = tend.shape
    stride = lat_rows + 1
    half = lat_rows // 2
    loads = [pltpu.make_async_copy(tend_ref.at[f], tend.at[f], in_sems.at[f]) for f in range(fields)]
    for load in loads:
        load.start()
    stores = []

    def send(block):
        part = pl.ds(block * half, half)
        store = pltpu.make_async_copy(rows.at[part], out_ref.at[part], out_sems.at[block])
        store.start()
        stores.append(store)

    def put(pair, *slots):
        slots = [squeeze(slot[:HEAD], slot[HEAD:]) for slot in slots]
        rows[pair] = jnp.concatenate(slots, axis=0).astype(jnp.bfloat16)

    def whole(f, r):
        return wide[f, pl.ds(r, SEG, stride=stride), :]

    def left(r):
        moved = [pltpu.roll(whole(f, r), (f + 1) * QUARTER, 1) for f in range(fields)]
        lane = lanes(moved[0])
        return jnp.where(lane < QUARTER, moved[0], jnp.where(lane < 2 * QUARTER, moved[1], moved[2]))

    for f in range(fields):
        wide[f, width * stride :] = jnp.zeros(((SEG - width) * stride, levels), jnp.float32)
    for f in range(fields):
        loads[f].wait()
        for q in range(width):
            wide[f, q * stride : q * stride + lat_rows] = tend[f, q].astype(jnp.float32)
        for r in range(half):
            put(f * half + r, whole(f, 2 * r), whole(f, 2 * r + 1))
        send(f)
    for r in range(half):
        put(fields * half + r, left(2 * r), left(2 * r + 1))
    send(fields)
    for store in stores:
        store.wait()


def transform_kernel(
    rows_ref, weight_ref, head_ref, tail_ref, out_ref, rows, result, in_sems, out_sems
):
    total, levels = rows.shape
    pairs = total // PAIR
    piece = total // LOADS
    loads = [
        pltpu.make_async_copy(
            rows_ref.at[pl.ds(i * piece, piece)], rows.at[pl.ds(i * piece, piece)], in_sems.at[i]
        )
        for i in range(LOADS)
    ]
    for load in loads:
        load.start()
    forward = (((0,), (0,)), ((), ()))
    back = (((1,), (1,)), ((), ()))
    spectrum = 0.0
    for i, load in enumerate(loads):
        load.wait()
        part = pl.ds(i * piece, piece)
        spectrum += lax.dot_general(
            rows[part], head_ref[part], forward, preferred_element_type=jnp.float32
        )
    tail = [tail_of(head) for head in halves(rows[...].astype(jnp.float32).reshape(pairs, PAIR, levels))]
    tail = jnp.concatenate(tail, axis=-2)
    tail = tail.reshape(tail_ref.shape[0], levels).astype(jnp.bfloat16)
    spectrum += lax.dot_general(tail, tail_ref[...], forward, preferred_element_type=jnp.float32)
    weighted = (spectrum * weight_ref[...]).astype(jnp.bfloat16)
    tail = lax.dot_general(tail_ref[...], weighted, back, preferred_element_type=jnp.float32)
    tail = tail.reshape(pairs, 2 * (SEG - HEAD), levels)
    count = pairs // CHUNKS
    stores = []
    for i in range(CHUNKS):
        part = pl.ds(i * count * PAIR, count * PAIR)
        head = lax.dot_general(head_ref[part], weighted, back, preferred_element_type=jnp.float32)
        head = halves(head.reshape(count, PAIR, levels))
        last = halves(tail[i * count : (i + 1) * count])
        head = jnp.concatenate([squeeze(h, t) for h, t in zip(head, last)], axis=-2)
        result[part] = head.reshape(count * PAIR, levels).astype(jnp.bfloat16)
        stores.append(pltpu.make_async_copy(result.at[part], out_ref.at[part], out_sems.at[i]))
        stores[i].start()
    for store in stores:
        store.wait()


def early_kernel(
    waiting,
    low_ref,
    factor_ref,
    tend_ref,
    wind_hbm,
    tracer_hbm,
    high_ref,
    side_ref,
    below_ref,
    top_ref,
    filt_hbm,
    out_hbm,
    first_ref,
    courant_ref,
    tracer_ref,
    *scratch,
):
    fields, _, lat_rows, _ = tend_ref.shape
    lat = lax.axis_index("lat")
    first_ref[0] = low_ref[lat_rows // 2]
    first_ref[1] = low_ref[fields * lat_rows // 2]
    add_scratch, advect_scratch = scratch[:6], scratch[6:]

    @pl.when(lat >= waiting)
    def _():
        loads = tracer_loads(tracer_hbm, tracer_ref, add_scratch[5])
        for load in loads[::-1]:
            load.start()
        stores = add_rows(
            lat, low_ref, factor_ref, tend_ref, wind_hbm, high_ref, filt_hbm, courant_ref, *add_scratch[:5]
        )
        advect(
            lat,
            factor_ref,
            courant_ref,
            tracer_ref,
            high_ref,
            side_ref,
            below_ref,
            top_ref,
            None,
            loads,
            out_hbm,
            *advect_scratch,
        )
        for store in stores:
            store.wait()


def middle_kernel(
    waiting,
    low_ref,
    factor_ref,
    tend_ref,
    wind_hbm,
    tracer_hbm,
    high_ref,
    _,
    filt_hbm,
    courant_ref,
    tracer_ref,
    *scratch,
):
    lat = lax.axis_index("lat")

    @pl.when(lat < waiting)
    def _():
        loads = tracer_loads(tracer_hbm, tracer_ref, scratch[5])
        for load in loads:
            load.start()
        stores = add_rows(
            lat, low_ref, factor_ref, tend_ref, wind_hbm, high_ref, filt_hbm, courant_ref, *scratch[:5]
        )
        for copy in loads + stores:
            copy.wait()


def late_kernel(
    waiting,
    factor_ref,
    courant_ref,
    tracer_ref,
    high_ref,
    side_ref,
    below_ref,
    top_ref,
    next_low_ref,
    _,
    out_hbm,
    *scratch,
):
    lat = lax.axis_index("lat")

    @pl.when(lat < waiting)
    def _():
        advect(
            lat,
            factor_ref,
            courant_ref,
            tracer_ref,
            high_ref,
            side_ref,
            below_ref,
            top_ref,
            next_low_ref,
            None,
            out_hbm,
            *scratch,
        )


def tracer_loads(tracer_hbm, tracer_ref, sems):
    return [
        pltpu.make_async_copy(
            tracer_hbm.at[:, pl.ds(i * COLS, COLS)], tracer_ref.at[:, pl.ds(i * COLS, COLS)], sems.at[i]
        )
        for i in range(tracer_ref.shape[1] // COLS)
    ]


def add_rows(
    lat,
    low_ref,
    factor_ref,
    tend_ref,
    wind_hbm,
    high_ref,
    filt_hbm,
    courant_ref,
    wide_ref,
    rest_ref,
    filt,
    wind_ref,
    sems,
):
    fields, width, lat_rows, levels = tend_ref.shape
    count = high_ref.shape[0] - 2
    stride = lat_rows + 1
    winds = [
        pltpu.make_async_copy(wind_hbm.at[f], wind_ref.at[f], sems.at[fields + f]) for f in range(2)
    ]
    for load in winds:
        load.start()
    stores = []
    damp = jnp.broadcast_to(factor_ref[lat, 0], (lat_rows, levels))

    half = lat_rows // 2
    for r in range(half):
        pair = expand(low_ref[fields * half + r].astype(jnp.float32))
        for i in range(2):
            rest_ref[2 * r + i] = pair[i]
    for f in range(fields):
        for r in range(half):
            pair = expand(low_ref[f * half + r].astype(jnp.float32))
            for i in range(2):
                row = with_rest(pair[i], rest_ref[2 * r + i], f)
                wide_ref[f, pl.ds(2 * r + i, SEG, stride=stride), :] = row
        for q in range(width):
            low = wide_ref[f, q * stride : q * stride + lat_rows]
            filt[f, q] = (damp * tend_ref[f, q].astype(jnp.float32) + low).astype(jnp.bfloat16)
        stores.append(pltpu.make_async_copy(filt.at[f], filt_hbm.at[f], sems.at[f]))
        stores[-1].start()
        if f < 2:
            winds[f].wait()
            courant_ref[f, :width] = (0.5, 0.25)[f] * jnp.tanh(wind_ref[f] + filt[f].astype(jnp.float32))
        if f == 0:
            edge = damp * high_ref[count + 1].astype(jnp.float32) + wide_ref[f, width * stride : width * stride + lat_rows]
            edge = edge.astype(jnp.bfloat16).astype(jnp.float32)
            courant_ref[f, width] = 0.5 * jnp.tanh(high_ref[count].astype(jnp.float32) + edge)
    return stores


def advect(
    lat,
    factor_ref,
    courant_ref,
    tracer_ref,
    high_ref,
    side_ref,
    below_ref,
    top_ref,
    next_low_ref,
    loads,
    out_hbm,
    out_ref,
    north_ref,
    below_wide,
    top_wide,
    sems,
):
    count, width, lat_rows, levels = tracer_ref.shape
    pieces = width // COLS
    stores = [
        pltpu.make_async_copy(
            out_ref.at[:, pl.ds(i * COLS, COLS)], out_hbm.at[:, pl.ds(i * COLS, COLS)], sems.at[i]
        )
        for i in range(pieces)
    ]
    face, face_next, inverse = (
        jnp.broadcast_to(factor_ref[lat, i], (lat_rows, levels)) for i in (1, 2, 3)
    )
    sublane = lax.broadcasted_iota(jnp.int32, (lat_rows, levels), 0)
    is_first = sublane == 0
    is_last = sublane == lat_rows - 1
    below_wide[:, :width] = below_ref[...].astype(jnp.float32)
    top_wide[:, :width] = top_ref[...].astype(jnp.float32)
    edge = factor_ref[lat, 4, 0:1] * below_wide[count + 1, :width]
    if next_low_ref is not None:
        row, rest = (expand(next_low_ref[i].astype(jnp.float32))[0] for i in range(2))
        edge += with_rest(row, rest, 1)[:width]
    edge = edge.astype(jnp.bfloat16).astype(jnp.float32)
    north_ref[:width] = 0.25 * jnp.tanh(below_wide[count, :width] + edge)
    if loads is not None:
        loads[pieces - 1].wait()
    east = courant_ref[0, width]
    flux = [
        jnp.maximum(east, 0.0) * tracer_ref[q, width - 1]
        + jnp.minimum(east, 0.0) * high_ref[q].astype(jnp.float32)
        for q in range(count)
    ]
    for piece in reversed(range(pieces)):
        if piece > 0 and loads is not None:
            loads[piece - 1].wait()
        for column in reversed(range(piece * COLS, (piece + 1) * COLS)):
            east = courant_ref[0, column]
            north = courant_ref[1, column]
            north_next = jnp.where(
                is_last, north_ref[column : column + 1], pltpu.roll(north, lat_rows - 1, 0)
            )
            west_plus = jnp.maximum(east, 0.0)
            west_minus = jnp.minimum(east, 0.0)
            pole_plus = face * jnp.maximum(north, 0.0)
            pole_minus = face * jnp.minimum(north, 0.0)
            next_plus = face_next * jnp.maximum(north_next, 0.0)
            next_minus = face_next * jnp.minimum(north_next, 0.0)
            for q in range(count):
                here = tracer_ref[q, column]
                if column > 0:
                    west = tracer_ref[q, column - 1]
                else:
                    west = side_ref[q].astype(jnp.float32)
                prior = jnp.where(
                    is_first, top_wide[q, column : column + 1], pltpu.roll(here, 1, 0)
                )
                after = jnp.where(
                    is_last, below_wide[q, column : column + 1], pltpu.roll(here, lat_rows - 1, 0)
                )
                f_west = west_plus * west + west_minus * here
                g_pole = pole_plus * prior + pole_minus * here
                g_next = next_plus * here + next_minus * after
                out_ref[q, column] = here - (flux[q] - f_west) - (g_next - g_pole) * inverse
                flux[q] = f_west
        stores[piece].start()
    for store in stores:
        store.wait()


def row_factors(lat_devices, lat_rows):
    ids = np.arange(lat_devices * lat_rows + 1)
    half = lat_devices * lat_rows // 2
    damping = np.where(ids < half, 0.25 + 0.5 * (ids + 0.5) / half, 1.0)
    grid_row = ids + HEMI // 2 - half
    face = np.sin(math.pi * grid_row / (2.0 * HEMI))
    centre = np.sin(math.pi * (grid_row + 0.5) / (2.0 * HEMI))
    rows = np.stack(
        [damping[:-1], face[:-1], face[1:], 1.0 / centre[:-1], np.repeat(damping[lat_rows::lat_rows], lat_rows)]
    )
    rows = rows.reshape(5, lat_devices, lat_rows).swapaxes(0, 1).astype(np.float32)
    return rows[..., None]


def in_vmem(array):
    return pltpu.with_memory_space_constraint(array, pltpu.VMEM)


def in_hbm(array):
    return pltpu.with_memory_space_constraint(array, pltpu.HBM)


def per_device(tendencies, bands, winds, tracers):
    fields, lat_rows, width, levels = tendencies.shape
    count = tracers.shape[0]
    lat_devices = lax.axis_size("lat")
    segments = lax.axis_size("lon")
    lat_place = lax.axis_index("lat")
    lon_place = lax.axis_index("lon")
    tendencies, winds, tracers = (a.transpose(0, 2, 1, 3) for a in (tendencies, winds, tracers))

    to_prior = [(i + 1, i) for i in range(lat_devices - 1)]
    to_next = [(i, i + 1) for i in range(lat_devices - 1)]
    west_ring = [((i + 1) % segments, i) for i in range(segments)]
    east_ring = [(i, (i + 1) % segments) for i in range(segments)]
    vmem = pl.BlockSpec(memory_space=pltpu.VMEM)
    hbm = pl.BlockSpec(memory_space=pltpu.HBM)
    params = pltpu.CompilerParams(vmem_limit_bytes=LIMIT)
    bf16 = jnp.bfloat16
    total = segments // 2 * PAIR
    sent = (segments, HEAD // 4, 4, levels)

    send = pl.pallas_call(
        pack_kernel,
        in_specs=[hbm],
        out_specs=hbm,
        out_shape=pltpu.HBM((segments // 2, PAIR, levels), bf16),
        scratch_shapes=[
            pltpu.VMEM(tendencies.shape, bf16),
            pltpu.VMEM((fields, SEG * (lat_rows + 1), levels), jnp.float32),
            pltpu.VMEM((segments // 2, PAIR, levels), bf16),
            pltpu.SemaphoreType.DMA((fields,)),
            pltpu.SemaphoreType.DMA((segments // lat_rows,)),
        ],
        compiler_params=params,
        name="pack",
    )(in_hbm(tendencies))
    with jax.named_scope("forth"):
        rows = lax.all_to_all(send.reshape(sent), "lon", split_axis=0, concat_axis=0, tiled=True)

    factors = jnp.asarray(row_factors(lat_devices, lat_rows))
    waves, _, used = wave_rows()
    row = lat_place * lat_rows + lon_place % lat_rows
    half = lat_devices * lat_rows // 2
    damping = 0.25 + 0.5 * (row.astype(jnp.float32) + 0.5) / half
    damping = jnp.where(row < half, damping, 1.0)
    fold = np.where(used, np.where(waves == 0, 1.0, 2.0), 0.0) / (segments * width)
    weight = (1.0 - damping) * jnp.asarray(fold, jnp.float32)[None]
    weight = jnp.where(jnp.asarray(waves)[None] <= bands[row], weight, 0.0)
    with jax.named_scope("table"):
        head_table, tail_table = (
            trig_table(segments * width, segments, order) for order in (HEAD_ORDER, TAIL_ORDER)
        )

    with jax.named_scope("edges"):
        high = jnp.concatenate(
            [tracers[:, 0].astype(bf16), winds[0:1, 0].astype(bf16), tendencies[0:1, 0]], axis=0
        )
        side = tracers[:, width - 1].astype(bf16)
        below = jnp.concatenate(
            [tracers[:, :, 0].astype(bf16), winds[1:2, :, 0].astype(bf16), tendencies[1:2, :, 0]], axis=0
        )
        top = tracers[:, :, lat_rows - 1].astype(bf16)
    with jax.named_scope("columns"):
        high = lax.ppermute(high, "lon", west_ring)
        side = lax.ppermute(side, "lon", east_ring)
    rows, head_table, tail_table, weight, high, side, below, top = lax.optimization_barrier(
        (rows, head_table, tail_table, weight, high, side, below, top)
    )

    low = pl.pallas_call(
        transform_kernel,
        in_specs=[hbm, vmem, vmem, vmem],
        out_specs=hbm,
        out_shape=pltpu.HBM((total, levels), bf16),
        scratch_shapes=[
            pltpu.VMEM((total, levels), bf16),
            pltpu.VMEM((total, levels), bf16),
            pltpu.SemaphoreType.DMA((LOADS,)),
            pltpu.SemaphoreType.DMA((CHUNKS,)),
        ],
        compiler_params=params,
        name="transform",
    )(
        in_hbm(rows.reshape(total, levels)),
        in_vmem(weight),
        in_vmem(head_table),
        in_vmem(tail_table),
    )
    low, below, top = lax.optimization_barrier((low, below, top))
    with jax.named_scope("back"):
        low = lax.all_to_all(
            low.reshape(sent), "lon", split_axis=0, concat_axis=0, tiled=True
        ).reshape(segments // 2, PAIR, levels)
    with jax.named_scope("below"):
        below = lax.ppermute(below, "lat", to_prior)
    with jax.named_scope("top"):
        top = lax.ppermute(top, "lat", to_next)
    waiting = lat_devices // 2 - 1
    filtered_out = pltpu.HBM(tendencies.shape, bf16)
    advected_out = pltpu.HBM(tracers.shape, jnp.float32)
    on_chip = [
        pltpu.VMEM((2, width + 1, lat_rows, levels), jnp.float32),
        pltpu.VMEM(tracers.shape, jnp.float32),
    ]
    add_scratch = [
        pltpu.VMEM((fields, SEG * (lat_rows + 1), levels), jnp.float32),
        pltpu.VMEM((lat_rows, SEG, levels), jnp.float32),
        pltpu.VMEM(tendencies.shape, bf16),
        pltpu.VMEM(winds.shape, jnp.float32),
        pltpu.SemaphoreType.DMA((fields + 2,)),
        pltpu.SemaphoreType.DMA((width // COLS,)),
    ]
    advect_scratch = [
        pltpu.VMEM(tracers.shape, jnp.float32),
        pltpu.VMEM((SEG, levels), jnp.float32),
        pltpu.VMEM((count + 2, SEG, levels), jnp.float32),
        pltpu.VMEM((count, SEG, levels), jnp.float32),
        pltpu.SemaphoreType.DMA((width // COLS,)),
    ]
    factors, high, side, below, top = (in_vmem(a) for a in (factors, high, side, below, top))
    operands = (in_vmem(low), factors, in_vmem(tendencies), in_hbm(winds), in_hbm(tracers), high)
    specs = [vmem] * 3 + [hbm] * 2 + [vmem]
    filtered, advected, first = pl.pallas_call(
        functools.partial(early_kernel, waiting),
        in_specs=specs + [vmem] * 3,
        out_specs=[hbm, hbm, vmem],
        out_shape=[filtered_out, advected_out, jax.ShapeDtypeStruct((2, PAIR, levels), bf16)],
        scratch_shapes=on_chip + add_scratch + advect_scratch,
        compiler_params=params,
        name="early",
    )(*operands, side, below, top)
    next_low = lax.ppermute(first, "lat", to_prior[:waiting])
    filtered, courant, held = pl.pallas_call(
        functools.partial(middle_kernel, waiting),
        in_specs=specs + [hbm],
        out_specs=[hbm, vmem, vmem],
        out_shape=[filtered_out] + on_chip,
        scratch_shapes=add_scratch,
        input_output_aliases={6: 0},
        compiler_params=params,
        name="middle",
    )(*operands, filtered)
    advected = pl.pallas_call(
        functools.partial(late_kernel, waiting),
        in_specs=[vmem] * 8 + [hbm],
        out_specs=hbm,
        out_shape=advected_out,
        scratch_shapes=advect_scratch,
        input_output_aliases={8: 0},
        compiler_params=params,
        name="late",
    )(factors, courant, held, high, side, below, top, in_vmem(next_low), advected)
    return (filtered.transpose(0, 2, 1, 3), advected.transpose(0, 2, 1, 3))


def solution(mesh):
    return jax.shard_map(
        per_device,
        mesh=mesh,
        in_specs=(
            P(None, "lat", "lon", None),
            P(),
            P(None, "lat", "lon", None),
            P(None, "lat", "lon", None),
        ),
        out_specs=(P(None, "lat", "lon", None), P(None, "lat", "lon", None)),
        check_vma=False,
    )
```
